32 devices in a mesh: member: 2 (over y), vec: 4 (over x, core), band: 4 (over z).
Axes of the slice: x: 2, y: 2, z: 4, core: 2. Of those that a mesh axis runs over, the one named last changes fastest.
Arguments:
- vectors: float32 [32, 3, 16, 1440], P(('member', 'vec'), None, 'band'), parts along dimension 0, may hold values from -6 to 6
- flow: float32 [4, 16, 1440], P(None, 'band'), may hold values from -1 to 1
- band_cut: int32 [16], replicated, may hold values from 2 to 127
- order: int32 [4], replicated, may hold values from 0 to 3, each once
Outputs:
- basis: float32 [32, 3, 16, 1440], P(('member', 'vec'), None, 'band'), parts along dimension 0
- growth: float32 [32], P(('member', 'vec')), parts along dimension 0
The draws below stay inside these ranges and needn't reach their ends.
There are 2 independent parts, one for each index of `member`. The reference program is written for one: setup_inputs(seed, part) draws one part's arguments, and reference() takes and returns one part's arrays. A program takes and returns all parts, laid end to end along the dimension named above; an argument that names none is the same for every part. Nothing has to cross between parts.
Inputs may be any that keep to these rules, and one draw needn't show every extreme that they name: `order`: each block number appears once.
All inputs are finite; a program needn't handle non-finite values.
Results may differ from the reference program's by a relative error of at most 0.0001.
Values sent between devices are 32-bit elements; how exact they have to be, the bound alone decides.
A program may use at most 64 MiB of HBM per device.

```python
import math
import jax
import jax.numpy as jnp
from jax import lax

NLON = 1440
KMAX = 128
VEC_DEV = 4
PAIRS = 1
CAP = 8
NLAT = 16
NVEC = 16
N_VEC = 4


def place_ends(result, own_key, smallest, largest):
    extent = result.shape
    place = [jax.random.randint(jax.random.fold_in(own_key, axis), (), 0, extent[axis]) for axis in range(len(extent))]
    result = result.at[tuple(place)].set(smallest)
    longest = extent.index(max(extent))
    place[longest] = (place[longest] + 1) % extent[longest]
    return result.at[tuple(place)].set(largest)


def levels(own_key, extent, split, least, top_value):
    def one(dim, parts):
        heights = jax.random.uniform(jax.random.fold_in(jax.random.fold_in(own_key, 6), dim), (parts,), jnp.float32, least / len(split), top_value / len(split))
        return jnp.repeat(jnp.exp(heights), extent[dim] // parts).reshape((-1,) + (1,) * (len(extent) - dim - 1))

    gain = one(*split[0])
    for cut in split[1:]:
        gain = gain * one(*cut)
    return gain


def scatter_about(stream_key, extent, scale, limit, shards=(), kind=jnp.bfloat16):
    loudness = levels(stream_key, extent, shards, -0.22, 0.18) if shards else 1.0
    values = jax.random.normal(stream_key, extent, jnp.float32) * scale * loudness
    return jnp.minimum(jnp.maximum(values, -limit), limit).astype(kind)


def setup_inputs(seed: int = 0, part: int = 0) -> dict:
    arg_keys = jax.random.split(jax.random.key(seed), 5)
    own_keys = jax.random.split(jax.random.fold_in(arg_keys[4], part), 5)
    vectors = scatter_about(own_keys[0], (NVEC, 3, NLAT, NLON), 1.0, 6.0, ((0, 4), (2, 4)), jnp.float32)
    flow = jnp.clip(jax.random.uniform(arg_keys[1], (4, NLAT, NLON), jnp.float32, -1.0, 1.0) * levels(arg_keys[1], (4, NLAT, NLON), ((1, 4),), -0.4, 0.0), -1.0, 1.0)
    band_cut = place_ends(jax.random.randint(arg_keys[2], (2 * CAP,), 2, KMAX), jax.random.fold_in(arg_keys[2], 1), 2, KMAX - 1).astype(jnp.int32)
    order = jax.random.permutation(arg_keys[3], N_VEC).astype(jnp.int32)
    return dict(vectors=vectors, flow=flow, band_cut=band_cut, order=order)


step_dt = 0.4
half_dt = 0.2
sixth_dt = 0.4 / 6.0

def tendency(z, coef):
    inner = z[:, :, 1:-1]
    dx = 0.5 * (jnp.roll(inner, -1, 3) - jnp.roll(inner, 1, 3))
    dy = 0.5 * (z[:, :, 2:] - z[:, :, :-2])
    speed_x = coef[0]
    speed_y = coef[1]
    depth = 1.0 + 0.5 * coef[2]
    rotation = 0.5 * coef[3]
    advect = -(speed_x * dx + speed_y * dy)
    t_height = advect[:, 0] - depth * (dx[:, 1] + dy[:, 2])
    t_zonal = advect[:, 1] - dx[:, 0] + rotation * inner[:, 2]
    t_merid = advect[:, 2] - dy[:, 0] - rotation * inner[:, 1]
    return jnp.stack([t_height, t_zonal, t_merid], 1)

def padded(state):
    return jnp.pad(state, ((0, 0), (0, 0), (1, 1), (0, 0)))

def rk_step(state, flow):
    k_one = tendency(padded(state), flow)
    k_two = tendency(padded(state + half_dt * k_one), flow)
    k_three = tendency(padded(state + half_dt * k_two), flow)
    k_four = tendency(padded(state + step_dt * k_three), flow)
    return state + sixth_dt * (k_one + 2.0 * k_two + 2.0 * k_three + k_four)

def mode_table(nlon, kmax):
    points = jnp.arange(nlon, dtype=jnp.int32)
    waves = jnp.arange(kmax, dtype=jnp.int32)
    phase = (waves[:, None] * points[None, :] % nlon).astype(jnp.float32) * (2.0 * math.pi / nlon)
    scale = jnp.where(waves == 0, math.sqrt(1.0 / nlon), math.sqrt(2.0 / nlon)).astype(jnp.float32)
    cosines = jnp.cos(phase) * scale[:, None]
    sines = jnp.sin(phase) * math.sqrt(2.0 / nlon)
    return jnp.concatenate([cosines, sines], 0)

def project(rows, cutoff, table, kmax):
    waves = jnp.arange(kmax, dtype=jnp.int32)
    wave_both = jnp.concatenate([waves, waves], 0)
    keep = (wave_both <= cutoff[..., None]).astype(jnp.float32)
    coeffs = jnp.einsum('...l,kl->...k', rows, table, precision=lax.Precision.HIGHEST)
    return jnp.einsum('...k,kl->...l', coeffs * keep, table, precision=lax.Precision.HIGHEST)

def polar_filter(state, band_cut, table):
    caps = jnp.concatenate([state[:, :, :CAP], state[:, :, NLAT - CAP:]], 2)
    done = project(caps, band_cut, table, KMAX)
    return jnp.concatenate([done[:, :, :CAP], state[:, :, CAP:NLAT - CAP], done[:, :, CAP:]], 2)

def reference(vectors, flow, band_cut, order):
    table = mode_table(NLON, KMAX)
    state = vectors
    for pair in range(PAIRS):
        for inner_step in range(2):
            state = rk_step(state, flow)
        state = polar_filter(state, band_cut, table)
    total = 3 * NLAT * NLON
    blocks = state.reshape(N_VEC, VEC_DEV, total)
    numbers = jnp.arange(N_VEC, dtype=jnp.int32)
    position = lax.optimization_barrier(jnp.sum(jnp.where(order[None, :] == numbers[:, None], numbers[None, :], 0), 1))
    growth = jnp.zeros((N_VEC, VEC_DEV), jnp.float32)
    for turn in range(N_VEC):
        panel = blocks[order[turn]]
        gram = jnp.dot(panel, panel.T, precision=lax.Precision.HIGHEST) / total
        lower = jnp.linalg.cholesky(gram)
        ortho = jax.scipy.linalg.solve_triangular(lower, panel, lower=True)
        coef = jnp.einsum('cvm,wm->cvw', blocks, ortho, precision=lax.Precision.HIGHEST) / total
        update = blocks - jnp.einsum('cvw,wm->cvm', coef, ortho, precision=lax.Precision.HIGHEST)
        later = (position > turn)[:, None, None]
        now = (position == turn)[:, None, None]
        blocks = jnp.where(later, update, jnp.where(now, ortho[None], blocks))
        growth = jnp.where(now[:, :, 0], jnp.log(jnp.diagonal(lower))[None, :], growth)
    return (blocks.reshape(NVEC, 3, NLAT, NLON), growth.reshape(NVEC))
```

```python
import math

import functools

import jax
import jax.numpy as jnp
import ml_dtypes
import numpy as np
from jax import lax
from jax.experimental import pallas as pl
from jax.experimental.pallas import tpu as pltpu
from jax.sharding import PartitionSpec as P

KMAX = 128
CAP_DEV = 2


step_dt = 0.4
half_dt = 0.2
sixth_dt = 0.4 / 6.0


def extended(block, sides, width):
    for axis, dim in sides:
        count = lax.axis_size(axis)
        forward = [(i, i + 1) for i in range(count - 1)]
        backward = [(target, source) for source, target in forward]
        low = lax.ppermute(
            lax.slice_in_dim(block, block.shape[dim] - width, None, axis=dim), axis, forward
        )
        high = lax.ppermute(lax.slice_in_dim(block, 0, width, axis=dim), axis, backward)
        block = jnp.concatenate([low, block, high], axis=dim)
    return block


def broadcast(value, axis, source):
    kept = jnp.where(lax.axis_index(axis) == source, value, 0).astype(value.dtype)
    return lax.psum(kept, axis)


def tendency(z, coef):
    inner = z[:, :, 1:-1]
    dx = 0.5 * (jnp.roll(inner, -1, 3) - jnp.roll(inner, 1, 3))
    dy = 0.5 * (z[:, :, 2:] - z[:, :, :-2])
    speed_x = coef[0]
    speed_y = coef[1]
    depth = 1.0 + 0.5 * coef[2]
    rotation = 0.5 * coef[3]
    advect = -(speed_x * dx + speed_y * dy)
    t_height = advect[:, 0] - depth * (dx[:, 1] + dy[:, 2])
    t_zonal = advect[:, 1] - dx[:, 0] + rotation * inner[:, 2]
    t_merid = advect[:, 2] - dy[:, 0] - rotation * inner[:, 1]
    return jnp.stack([t_height, t_zonal, t_merid], 1)


def with_rows(state):
    return extended(state, (("band", 2),), 1)


def step_near(state, flow):
    k_one = tendency(with_rows(state), flow)
    k_two = tendency(with_rows(state + half_dt * k_one), flow)
    k_three = tendency(with_rows(state + half_dt * k_two), flow)
    k_four = tendency(with_rows(state + step_dt * k_three), flow)
    return state + sixth_dt * (k_one + 2.0 * k_two + 2.0 * k_three + k_four)


def mode_table(nlon, kmax):
    points = jnp.arange(nlon, dtype=jnp.int32)
    waves = jnp.arange(kmax, dtype=jnp.int32)
    phase = (waves[:, None] * points[None, :] % nlon).astype(jnp.float32) * (2.0 * math.pi / nlon)
    scale = jnp.where(waves == 0, math.sqrt(1.0 / nlon), math.sqrt(2.0 / nlon)).astype(jnp.float32)
    cosines = jnp.cos(phase) * scale[:, None]
    sines = jnp.sin(phase) * math.sqrt(2.0 / nlon)
    return jnp.concatenate([cosines, sines], 0)


def project(rows, cutoff, table, kmax):
    waves = jnp.arange(kmax, dtype=jnp.int32)
    wave_both = jnp.concatenate([waves, waves], 0)
    keep = (wave_both <= cutoff[..., None]).astype(jnp.float32)
    coeffs = jnp.einsum("...l,kl->...k", rows, table, precision=lax.Precision.HIGHEST)
    return jnp.einsum("...k,kl->...l", coeffs * keep, table, precision=lax.Precision.HIGHEST)


def polar_filter(state, band_cut, table):
    nband = lax.axis_size("band")
    me_band = lax.axis_index("band")
    lat_dev = state.shape[2]
    cap_rows = CAP_DEV * lat_dev
    north = me_band < CAP_DEV
    south = me_band >= nband - CAP_DEV
    start = jnp.where(north, me_band * lat_dev, cap_rows + (me_band - nband + CAP_DEV) * lat_dev)
    start = jnp.clip(start, 0, 2 * cap_rows - lat_dev)
    cutoff = lax.dynamic_slice_in_dim(band_cut, start, lat_dev)
    return lax.cond(
        north | south, lambda value: project(value, cutoff, table, KMAX), lambda value: value, state
    )


def on_device(vectors, flow, band_cut, order):
    state = vectors
    nband = lax.axis_size("band")
    lat_dev = state.shape[2]
    table = mode_table(state.shape[3], KMAX)
    for inner_step in range(2):
        state = step_near(state, flow)
    state = polar_filter(state, band_cut, table)
    nblocks = lax.axis_size("vec")
    me_vec = lax.axis_index("vec")
    vec_dev = state.shape[0]
    total = float(3 * nband * lat_dev * state.shape[3])
    flat = state.reshape(vec_dev, -1)
    numbers = jnp.arange(nblocks, dtype=jnp.int32)
    position = jnp.sum(jnp.where(order == me_vec, numbers, 0))
    growth = jnp.zeros((vec_dev,), jnp.float32)
    for turn in range(nblocks):
        panel = broadcast(flat, "vec", order[turn])
        gram = lax.psum(jnp.dot(panel, panel.T, precision=lax.Precision.HIGHEST), "band") / total
        lower = jnp.linalg.cholesky(gram)
        ortho = jax.scipy.linalg.solve_triangular(lower, panel, lower=True)
        coef = lax.psum(jnp.dot(flat, ortho.T, precision=lax.Precision.HIGHEST), "band") / total
        update = flat - jnp.dot(coef, ortho, precision=lax.Precision.HIGHEST)
        flat = jnp.where(position > turn, update, jnp.where(position == turn, ortho, flat))
        growth = jnp.where(position == turn, jnp.log(jnp.diagonal(lower)), growth)
    return (flat.reshape(state.shape), growth)


MESH = pl.DeviceIdType.MESH
HIGHEST = lax.Precision.HIGHEST
GROUP = 4
NUM = GROUP * GROUP


def split_table(nlon, kmax, width):
    waves = np.arange(kmax)[:, None]
    phase = (waves * np.arange(nlon)[None, :] % nlon) * (2.0 * np.pi / nlon)
    scale = np.where(waves == 0, np.sqrt(1.0 / nlon), np.sqrt(2.0 / nlon))
    table = np.concatenate([np.cos(phase) * scale, np.sin(phase) * np.sqrt(2.0 / nlon)], 0)
    table = table.astype(np.float32)
    high = table.astype(ml_dtypes.bfloat16)
    low = (table - high.astype(np.float32)).astype(ml_dtypes.bfloat16)
    rows = ((0, width - nlon), (0, 0))
    return np.stack([high, low]), np.stack([np.pad(high.T, rows), np.pad(low.T, rows)])


def halves(value):
    high = value.astype(jnp.bfloat16)
    return high, (value - high.astype(jnp.float32)).astype(jnp.bfloat16)


def dot_split(value, table_ref):
    high, low = halves(value)
    dot = functools.partial(jnp.dot, preferred_element_type=jnp.float32)
    return dot(high, table_ref[0]) + (dot(low, table_ref[0]) + dot(high, table_ref[1]))


def dot_full(left, right):
    return jnp.dot(left, right, precision=HIGHEST, preferred_element_type=jnp.float32)


def iota(shape, dim):
    return lax.broadcasted_iota(jnp.int32, shape, dim)


def tend_rows(h, u, v, coef):
    neg_u, neg_v, neg_h, rot = coef
    rows, width = h.shape
    row = iota((rows, width), 0)

    def along_x(z):
        return pltpu.roll(z, width - 1, 1) - pltpu.roll(z, 1, 1)

    def along_y(z):
        above = jnp.where(row == rows - 1, 0.0, pltpu.roll(z, rows - 1, 0))
        below = jnp.where(row == 0, 0.0, pltpu.roll(z, 1, 0))
        return above - below

    xh, xu, xv = along_x(h), along_x(u), along_x(v)
    yh, yu, yv = along_y(h), along_y(u), along_y(v)
    th = neg_u * xh + neg_v * yh + neg_h * (xu + yv)
    tu = neg_u * xu + neg_v * yu - 0.5 * xh + rot * v
    tv = neg_u * xv + neg_v * yv - 0.5 * yh - rot * u
    return th, tu, tv


def step_rows(x, coef):
    k = tend_rows(*x, coef)
    total = k
    for scale, weight in ((half_dt, 2.0), (half_dt, 2.0), (step_dt, 1.0)):
        k = tend_rows(*[a + scale * b for a, b in zip(x, k)], coef)
        total = [a + weight * b for a, b in zip(total, k)]
    return [a + sixth_dt * b for a, b in zip(x, total)]


def whole_kernel(
    nlon, width, size,
    order_ref, cut_ref, vec_hbm, flow_hbm, fwd_hbm, inv_hbm,
    out_ref, growth_ref,
    vbuf, fbuf, fwd, inv, xs, fs, sbuf, cs, gsend, gbuf, nb,
    local_sem, vsend, vrecv, fsend, frecv, gosend, gorecv, csend, crecv, asend, arecv, msend, mrecv,
):
    b = lax.axis_index("band")
    v = lax.axis_index("vec")

    def peer(k):
        return lax.rem(b + k // GROUP, GROUP), lax.rem(v + k % GROUP, GROUP)

    def remote(src, dst, send, recv, b2, v2):
        return pltpu.make_async_remote_copy(
            src_ref=src, dst_ref=dst, send_sem=send, recv_sem=recv,
            device_id={"band": b2, "vec": v2}, device_id_type=MESH,
        )

    own = [
        pltpu.make_async_copy(flow_hbm.at[v], fbuf.at[v, b], local_sem.at[0]),
        pltpu.make_async_copy(vec_hbm.at[b], vbuf.at[b], local_sem.at[1]),
        pltpu.make_async_copy(fwd_hbm, fwd, local_sem.at[2]),
        pltpu.make_async_copy(inv_hbm, inv, local_sem.at[3]),
    ]
    for copy in own:
        copy.start()

    barrier = pltpu.get_barrier_semaphore()
    for k in range(1, NUM):
        b2, v2 = peer(k)
        pl.semaphore_signal(barrier, inc=1, device_id={"band": b2, "vec": v2}, device_id_type=MESH)
    pl.semaphore_wait(barrier, NUM - 1)

    flow_copies, vec_copies = [], []
    for k in range(1, GROUP):
        b2 = lax.rem(b + k, GROUP)
        flow_copies.append(
            remote(flow_hbm.at[v], fbuf.at[v, b], fsend.at[k], frecv.at[k], b2, v)
        )
        flow_copies[-1].start()
    for k in range(1, GROUP):
        b2 = lax.rem(b + k, GROUP)
        vec_copies.append(remote(vec_hbm.at[b2], vbuf.at[b], vsend.at[k], vrecv.at[k], b2, v))
        vec_copies[-1].start()

    lane = iota((NUM, 128), 1)
    row = iota((NUM, 128), 0)

    def placed(at):
        turn = at // GROUP
        block = jnp.where(
            turn == 0, order_ref[0],
            jnp.where(turn == 1, order_ref[1], jnp.where(turn == 2, order_ref[2], order_ref[3])),
        )
        return GROUP * block + at % GROUP

    permute = (lane == placed(row)).astype(jnp.float32)
    lane_big = iota((128, 128), 1)
    row_big = iota((128, 128), 0)
    unpack = (
        (row_big % NUM == placed(lane_big - NUM)) & (lane_big >= NUM) & (lane_big < 2 * NUM)
    ).astype(jnp.float32)
    diagonal = lane // NUM == row % 8
    own_rows = (placed(lane[:8]) == GROUP * v + row[:8]) & (lane[:8] < NUM) & (row[:8] < GROUP)
    own_rows = own_rows.astype(jnp.float32)
    wave = iota((NUM, 2 * KMAX), 1) % KMAX
    wave_row = iota((NUM, 2 * KMAX), 0)
    cut = jnp.zeros((NUM, 2 * KMAX), jnp.int32)
    for r in range(NUM):
        cut = jnp.where(wave_row == r, cut_ref[r], cut)
    keep = wave <= cut

    own[0].wait()
    for copy in flow_copies:
        copy.wait_recv()
    forwards = []
    for k in range(1, GROUP):
        v2 = lax.rem(v + k, GROUP)
        forwards.append(remote(fbuf.at[v], fbuf.at[v], gosend.at[k], gorecv.at[k], b, v2))
        forwards[-1].start()

    own[1].wait()
    for copy in vec_copies:
        copy.wait_recv()
    for copy in forwards:
        copy.wait_recv()

    extra = width - nlon
    for f in range(3):
        for band in range(GROUP):
            xs[f, GROUP * band : GROUP * (band + 1), :nlon] = vbuf[band, f]
    for f in range(GROUP):
        for band in range(GROUP):
            fs[f, GROUP * band : GROUP * (band + 1), :nlon] = fbuf[f, band]

    def wrapped(z):
        return jnp.concatenate([z, z[:, : extra // 2], z[:, nlon - extra // 2 :]], axis=1)

    x = [wrapped(xs[f, :, :nlon]) for f in range(3)]
    speed_x, speed_y, deep, turning = [wrapped(fs[f, :, :nlon]) for f in range(GROUP)]
    coef = (-0.5 * speed_x, -0.5 * speed_y, -0.5 - 0.25 * deep, 0.5 * turning)
    for _ in range(2):
        x = step_rows(x, coef)

    own[2].wait()
    modes = dot_split(jnp.concatenate(x, axis=0), fwd)
    for f in range(3):
        kept = jnp.where(keep, modes[NUM * f : NUM * (f + 1)], 0.0)
        sbuf[:, 0, 2 * KMAX * f : 2 * KMAX * (f + 1)] = kept

    me = GROUP * v + b
    mode_copies = []
    for k in range(1, NUM):
        b2, v2 = peer(k)
        mode_copies.append(
            remote(sbuf.at[GROUP * b2 + v2], cs.at[v2, me], csend.at[k], crecv.at[k], b2, v2)
        )
        mode_copies[-1].start()
    cs[v, me] = sbuf[GROUP * b + v]
    for copy in mode_copies:
        copy.wait_recv()

    gathers = []
    for k in range(1, GROUP):
        v2 = lax.rem(v + k, GROUP)
        gathers.append(remote(cs.at[v], cs.at[v], asend.at[k], arecv.at[k], b, v2))

    part = cs[v].reshape(NUM, 6 * KMAX)
    tiled = jnp.concatenate([part] * 8, axis=0)
    product = lax.dot_general(
        part, tiled, (((1,), (1,)), ((), ())), precision=HIGHEST,
        preferred_element_type=jnp.float32,
    )
    product = jnp.where(diagonal, product, 0.0)
    gsend[0:1, :] = jnp.sum(product[:8], axis=0, keepdims=True)
    gsend[1:2, :] = jnp.sum(product[8:], axis=0, keepdims=True)
    gram_copies = []
    for k in range(1, NUM):
        b2, v2 = peer(k)
        gram_copies.append(remote(gsend, gbuf.at[me], msend.at[k], mrecv.at[k], b2, v2))
        gram_copies[-1].start()
    for copy in gathers:
        copy.start()
    gbuf[me] = gsend[...]
    for copy in gram_copies:
        copy.wait_recv()
    gram = gbuf[0]
    for k in range(1, NUM):
        gram = gram + gbuf[k]
    gram = gram * (1.0 / size)
    spread = jnp.concatenate(
        [jnp.broadcast_to(gram[i : i + 1], (8, 128)) for i in range(2)], axis=0
    )
    spread = jnp.where(diagonal, spread, 0.0)
    grid = dot_full(permute[:, :NUM], dot_full(spread, unpack))
    grid = jnp.where(lane < NUM, permute, grid)
    for s in range(NUM - 1):
        col = grid[:, NUM + s : NUM + s + 1]
        factor = col / grid[s : s + 1, NUM + s : NUM + s + 1]
        grid = grid - jnp.where(row > s, factor * grid[s : s + 1, :], 0.0)
    pivot = jnp.sum(jnp.where(lane == row + NUM, grid, 0.0), axis=1, keepdims=True)
    root = jnp.sqrt(pivot)
    logs = jnp.broadcast_to(jnp.log(root), (NUM, 128))
    mix = jnp.where(lane < NUM, grid / root, logs)
    mix = dot_full(own_rows[:, :NUM], mix)
    for i in range(GROUP):
        growth_ref[i] = mix[i, NUM]

    for copy in gathers:
        copy.wait_recv()
    for r in range(GROUP):
        fresh = dot_full(mix[:, :NUM], cs[r].reshape(NUM, 6 * KMAX))
        for i in range(GROUP):
            for f in range(3):
                at = 12 * i + GROUP * f + r
                nb[at : at + 1, :] = fresh[i : i + 1, 2 * KMAX * f : 2 * KMAX * (f + 1)]
    own[3].wait()
    result = dot_split(nb[...], inv)
    for i in range(GROUP):
        for f in range(3):
            at = 12 * i + GROUP * f
            out_ref[i, f] = result[at : at + GROUP]

    for copy in flow_copies + vec_copies + forwards + mode_copies + gathers + gram_copies:
        copy.wait_send()


def on_group(vectors, flow, band_cut, order):
    nlon = vectors.shape[3]
    width = -(-nlon // 128) * 128
    inv, fwd = split_table(nlon, KMAX, width)
    any_spec = pl.BlockSpec(memory_space=pl.ANY)
    smem = pl.BlockSpec(memory_space=pltpu.SMEM)
    dma = pltpu.SemaphoreType.DMA
    size = float(3 * NUM * nlon)
    return tuple(pl.pallas_call(
        functools.partial(whole_kernel, nlon, width, size),
        out_shape=[
            jax.ShapeDtypeStruct(vectors.shape, jnp.float32),
            jax.ShapeDtypeStruct((GROUP,), jnp.float32),
        ],
        in_specs=[smem, smem, any_spec, any_spec, any_spec, any_spec],
        out_specs=[pl.BlockSpec(memory_space=pltpu.VMEM), smem],
        scratch_shapes=[
            pltpu.VMEM((GROUP, 3, GROUP, nlon), jnp.float32),
            pltpu.VMEM((GROUP, GROUP, GROUP, nlon), jnp.float32),
            pltpu.VMEM(fwd.shape, jnp.bfloat16),
            pltpu.VMEM(inv.shape, jnp.bfloat16),
            pltpu.VMEM((3, NUM, width), jnp.float32),
            pltpu.VMEM((GROUP, NUM, width), jnp.float32),
            pltpu.VMEM((NUM, 1, 6 * KMAX), jnp.float32),
            pltpu.VMEM((GROUP, NUM, 1, 6 * KMAX), jnp.float32),
            pltpu.VMEM((2, 128), jnp.float32),
            pltpu.VMEM((NUM, 2, 128), jnp.float32),
            pltpu.VMEM((3 * NUM, 2 * KMAX), jnp.float32),
            dma((4,)),
            dma((GROUP,)), dma((GROUP,)), dma((GROUP,)), dma((GROUP,)), dma((GROUP,)), dma((GROUP,)),
            dma((NUM,)), dma((NUM,)), dma((GROUP,)), dma((GROUP,)), dma((NUM,)), dma((NUM,)),
        ],
        compiler_params=pltpu.CompilerParams(
            collective_id=0, has_side_effects=True, vmem_limit_bytes=40 << 20
        ),
    )(order, band_cut, vectors, flow, jnp.asarray(fwd), jnp.asarray(inv)))


def solution(mesh):
    in_specs = (P(("member", "vec"), None, "band", None), P(None, "band", None), P(), P())
    out_specs = (P(("member", "vec"), None, "band", None), P(("member", "vec")))

    def body(vectors, flow, band_cut, order):
        rows = mesh.shape["band"] * vectors.shape[2]
        square = (mesh.shape["band"], mesh.shape["vec"], vectors.shape[0], vectors.shape[2])
        if rows == band_cut.shape[0] and square == (GROUP,) * 4:
            return on_group(vectors, flow, band_cut, order)
        return on_device(vectors, flow, band_cut, order)

    return jax.shard_map(
        body, mesh=mesh, in_specs=in_specs, out_specs=out_specs, check_vma=False
    )
```

```python
import math

import functools

import jax
import jax.numpy as jnp
import ml_dtypes
import numpy as np
from jax import lax
from jax.experimental import pallas as pl
from jax.experimental.pallas import tpu as pltpu
from jax.sharding import PartitionSpec as P

KMAX = 128
CAP_DEV = 2


step_dt = 0.4
half_dt = 0.2
sixth_dt = 0.4 / 6.0


def extended(block, sides, width):
    for axis, dim in sides:
        count = lax.axis_size(axis)
        forward = [(i, i + 1) for i in range(count - 1)]
        backward = [(target, source) for source, target in forward]
        low = lax.ppermute(
            lax.slice_in_dim(block, block.shape[dim] - width, None, axis=dim), axis, forward
        )
        high = lax.ppermute(lax.slice_in_dim(block, 0, width, axis=dim), axis, backward)
        block = jnp.concatenate([low, block, high], axis=dim)
    return block


def broadcast(value, axis, source):
    kept = jnp.where(lax.axis_index(axis) == source, value, 0).astype(value.dtype)
    return lax.psum(kept, axis)


def tendency(z, coef):
    inner = z[:, :, 1:-1]
    dx = 0.5 * (jnp.roll(inner, -1, 3) - jnp.roll(inner, 1, 3))
    dy = 0.5 * (z[:, :, 2:] - z[:, :, :-2])
    speed_x = coef[0]
    speed_y = coef[1]
    depth = 1.0 + 0.5 * coef[2]
    rotation = 0.5 * coef[3]
    advect = -(speed_x * dx + speed_y * dy)
    t_height = advect[:, 0] - depth * (dx[:, 1] + dy[:, 2])
    t_zonal = advect[:, 1] - dx[:, 0] + rotation * inner[:, 2]
    t_merid = advect[:, 2] - dy[:, 0] - rotation * inner[:, 1]
    return jnp.stack([t_height, t_zonal, t_merid], 1)


def with_rows(state):
    return extended(state, (("band", 2),), 1)


def step_near(state, flow):
    k_one = tendency(with_rows(state), flow)
    k_two = tendency(with_rows(state + half_dt * k_one), flow)
    k_three = tendency(with_rows(state + half_dt * k_two), flow)
    k_four = tendency(with_rows(state + step_dt * k_three), flow)
    return state + sixth_dt * (k_one + 2.0 * k_two + 2.0 * k_three + k_four)


def mode_table(nlon, kmax):
    points = jnp.arange(nlon, dtype=jnp.int32)
    waves = jnp.arange(kmax, dtype=jnp.int32)
    phase = (waves[:, None] * points[None, :] % nlon).astype(jnp.float32) * (2.0 * math.pi / nlon)
    scale = jnp.where(waves == 0, math.sqrt(1.0 / nlon), math.sqrt(2.0 / nlon)).astype(jnp.float32)
    cosines = jnp.cos(phase) * scale[:, None]
    sines = jnp.sin(phase) * math.sqrt(2.0 / nlon)
    return jnp.concatenate([cosines, sines], 0)


def project(rows, cutoff, table, kmax):
    waves = jnp.arange(kmax, dtype=jnp.int32)
    wave_both = jnp.concatenate([waves, waves], 0)
    keep = (wave_both <= cutoff[..., None]).astype(jnp.float32)
    coeffs = jnp.einsum("...l,kl->...k", rows, table, precision=lax.Precision.HIGHEST)
    return jnp.einsum("...k,kl->...l", coeffs * keep, table, precision=lax.Precision.HIGHEST)


def polar_filter(state, band_cut, table):
    nband = lax.axis_size("band")
    me_band = lax.axis_index("band")
    lat_dev = state.shape[2]
    cap_rows = CAP_DEV * lat_dev
    north = me_band < CAP_DEV
    south = me_band >= nband - CAP_DEV
    start = jnp.where(north, me_band * lat_dev, cap_rows + (me_band - nband + CAP_DEV) * lat_dev)
    start = jnp.clip(start, 0, 2 * cap_rows - lat_dev)
    cutoff = lax.dynamic_slice_in_dim(band_cut, start, lat_dev)
    return lax.cond(
        north | south, lambda value: project(value, cutoff, table, KMAX), lambda value: value, state
    )


def on_device(vectors, flow, band_cut, order):
    state = vectors
    nband = lax.axis_size("band")
    lat_dev = state.shape[2]
    table = mode_table(state.shape[3], KMAX)
    for inner_step in range(2):
        state = step_near(state, flow)
    state = polar_filter(state, band_cut, table)
    nblocks = lax.axis_size("vec")
    me_vec = lax.axis_index("vec")
    vec_dev = state.shape[0]
    total = float(3 * nband * lat_dev * state.shape[3])
    flat = state.reshape(vec_dev, -1)
    numbers = jnp.arange(nblocks, dtype=jnp.int32)
    position = jnp.sum(jnp.where(order == me_vec, numbers, 0))
    growth = jnp.zeros((vec_dev,), jnp.float32)
    for turn in range(nblocks):
        panel = broadcast(flat, "vec", order[turn])
        gram = lax.psum(jnp.dot(panel, panel.T, precision=lax.Precision.HIGHEST), "band") / total
        lower = jnp.linalg.cholesky(gram)
        ortho = jax.scipy.linalg.solve_triangular(lower, panel, lower=True)
        coef = lax.psum(jnp.dot(flat, ortho.T, precision=lax.Precision.HIGHEST), "band") / total
        update = flat - jnp.dot(coef, ortho, precision=lax.Precision.HIGHEST)
        flat = jnp.where(position > turn, update, jnp.where(position == turn, ortho, flat))
        growth = jnp.where(position == turn, jnp.log(jnp.diagonal(lower)), growth)
    return (flat.reshape(state.shape), growth)


MESH = pl.DeviceIdType.MESH
HIGHEST = lax.Precision.HIGHEST
GROUP = 4
NUM = GROUP * GROUP


def split_table(nlon, kmax, width):
    waves = np.arange(kmax)[:, None]
    phase = (waves * np.arange(nlon)[None, :] % nlon) * (2.0 * np.pi / nlon)
    scale = np.where(waves == 0, np.sqrt(1.0 / nlon), np.sqrt(2.0 / nlon))
    table = np.concatenate([np.cos(phase) * scale, np.sin(phase) * np.sqrt(2.0 / nlon)], 0)
    table = table.astype(np.float32)
    high = table.astype(ml_dtypes.bfloat16)
    low = (table - high.astype(np.float32)).astype(ml_dtypes.bfloat16)
    rows = ((0, width - nlon), (0, 0))
    return np.stack([high, low]), np.stack([np.pad(high.T, rows), np.pad(low.T, rows)])


def halves(value):
    high = value.astype(jnp.bfloat16)
    return high, (value - high.astype(jnp.float32)).astype(jnp.bfloat16)


def dot_split(value, table_ref):
    high, low = halves(value)
    dot = functools.partial(jnp.dot, preferred_element_type=jnp.float32)
    return dot(high, table_ref[0]) + (dot(low, table_ref[0]) + dot(high, table_ref[1]))


def dot_full(left, right):
    return jnp.dot(left, right, precision=HIGHEST, preferred_element_type=jnp.float32)


def iota(shape, dim):
    return lax.broadcasted_iota(jnp.int32, shape, dim)


def tend_rows(h, u, v, coef):
    neg_u, neg_v, neg_h, rot = coef
    rows, width = h.shape
    row = iota((rows, width), 0)

    def along_x(z):
        return pltpu.roll(z, width - 1, 1) - pltpu.roll(z, 1, 1)

    def along_y(z):
        above = jnp.where(row == rows - 1, 0.0, pltpu.roll(z, rows - 1, 0))
        below = jnp.where(row == 0, 0.0, pltpu.roll(z, 1, 0))
        return above - below

    xh, xu, xv = along_x(h), along_x(u), along_x(v)
    yh, yu, yv = along_y(h), along_y(u), along_y(v)
    th = neg_u * xh + neg_v * yh + neg_h * (xu + yv)
    tu = neg_u * xu + neg_v * yu - 0.5 * xh + rot * v
    tv = neg_u * xv + neg_v * yv - 0.5 * yh - rot * u
    return th, tu, tv


def step_rows(x, coef):
    k = tend_rows(*x, coef)
    total = k
    for scale, weight in ((half_dt, 2.0), (half_dt, 2.0), (step_dt, 1.0)):
        k = tend_rows(*[a + scale * b for a, b in zip(x, k)], coef)
        total = [a + weight * b for a, b in zip(total, k)]
    return [a + sixth_dt * b for a, b in zip(x, total)]


def whole_kernel(
    nlon, width, size,
    order_hbm, cut_hbm, vec_hbm, flow_hbm, fwd_hbm,
    nb, mix_ref,
    order_ref, cut_ref, vbuf, fbuf, fwd, xs, fs, sbuf, cs, gsend, gbuf,
    local_sem, vsend, vrecv, fsend, frecv, gosend, gorecv, csend, crecv, asend, arecv, msend, mrecv,
):
    b = lax.axis_index("band")
    v = lax.axis_index("vec")

    def remote(src, dst, send, recv, b2, v2):
        return pltpu.make_async_remote_copy(
            src_ref=src, dst_ref=dst, send_sem=send, recv_sem=recv,
            device_id={"band": b2, "vec": v2}, device_id_type=MESH,
        )

    own = [
        pltpu.make_async_copy(flow_hbm.at[v], fbuf.at[v, b], local_sem.at[0]),
        pltpu.make_async_copy(vec_hbm.at[b], vbuf.at[b], local_sem.at[1]),
        pltpu.make_async_copy(fwd_hbm, fwd, local_sem.at[2]),
        pltpu.make_async_copy(order_hbm, order_ref, local_sem.at[3]),
        pltpu.make_async_copy(cut_hbm, cut_ref, local_sem.at[4]),
    ]
    for copy in own:
        copy.start()

    barrier = pltpu.get_barrier_semaphore()
    bands = [lax.rem(b + k, GROUP) for k in range(GROUP)]
    vecs = [lax.rem(v + k, GROUP) for k in range(GROUP)]
    for b2, v2 in [(b2, v) for b2 in bands[1:]] + [(b, v2) for v2 in vecs[1:]]:
        pl.semaphore_signal(barrier, inc=1, device_id={"band": b2, "vec": v2}, device_id_type=MESH)
    pl.semaphore_wait(barrier, 2 * GROUP - 2)

    flow_copies, vec_copies = [], []
    for k in range(1, GROUP):
        b2 = bands[k]
        flow_copies.append(
            remote(flow_hbm.at[v], fbuf.at[v, b], fsend.at[k], frecv.at[k], b2, v)
        )
        flow_copies[-1].start()
    for k in range(1, GROUP):
        b2 = bands[k]
        vec_copies.append(remote(vec_hbm.at[b2], vbuf.at[b], vsend.at[k], vrecv.at[k], b2, v))
        vec_copies[-1].start()

    own[3].wait()
    own[4].wait()
    lane = iota((NUM, 128), 1)
    row = iota((NUM, 128), 0)

    def placed(at):
        turn = at // GROUP
        block = jnp.where(
            turn == 0, order_ref[0],
            jnp.where(turn == 1, order_ref[1], jnp.where(turn == 2, order_ref[2], order_ref[3])),
        )
        return GROUP * block + at % GROUP

    permute = (lane == placed(row)).astype(jnp.float32)
    lane_big = iota((128, 128), 1)
    row_big = iota((128, 128), 0)
    unpack = (
        (row_big % NUM == placed(lane_big - NUM)) & (lane_big >= NUM) & (lane_big < 2 * NUM)
    ).astype(jnp.float32)
    diagonal = lane // NUM == row % 8
    own_rows = (placed(lane[:8]) == GROUP * v + row[:8]) & (lane[:8] < NUM) & (row[:8] < GROUP)
    own_rows = own_rows.astype(jnp.float32)
    wave = iota((NUM, 2 * KMAX), 1) % KMAX
    wave_row = iota((NUM, 2 * KMAX), 0)
    cut = jnp.zeros((NUM, 2 * KMAX), jnp.int32)
    for r in range(NUM):
        cut = jnp.where(wave_row == r, cut_ref[r], cut)
    keep = wave <= cut

    own[0].wait()
    for copy in flow_copies:
        copy.wait_recv()
    forwards = []
    for k in range(1, GROUP):
        v2 = vecs[k]
        forwards.append(remote(fbuf.at[v], fbuf.at[v], gosend.at[k], gorecv.at[k], b, v2))
        forwards[-1].start()

    own[1].wait()
    for copy in vec_copies:
        copy.wait_recv()
    for copy in forwards:
        copy.wait_recv()

    extra = width - nlon
    for f in range(3):
        for band in range(GROUP):
            xs[f, GROUP * band : GROUP * (band + 1), :nlon] = vbuf[band, f]
    for f in range(GROUP):
        for band in range(GROUP):
            fs[f, GROUP * band : GROUP * (band + 1), :nlon] = fbuf[f, band]

    def wrapped(z):
        return jnp.concatenate([z, z[:, : extra // 2], z[:, nlon - extra // 2 :]], axis=1)

    x = [wrapped(xs[f, :, :nlon]) for f in range(3)]
    speed_x, speed_y, deep, turning = [wrapped(fs[f, :, :nlon]) for f in range(GROUP)]
    coef = (-0.5 * speed_x, -0.5 * speed_y, -0.5 - 0.25 * deep, 0.5 * turning)
    for _ in range(2):
        x = step_rows(x, coef)

    own[2].wait()
    modes = dot_split(jnp.concatenate(x, axis=0), fwd)
    for f in range(3):
        kept = jnp.where(keep, modes[NUM * f : NUM * (f + 1)], 0.0)
        sbuf[:, 0, 2 * KMAX * f : 2 * KMAX * (f + 1)] = kept

    mode_copies = []
    for k in range(1, GROUP):
        b2 = bands[k]
        rows = pl.ds(pl.multiple_of(GROUP * b2, GROUP), GROUP)
        mode_copies.append(remote(sbuf.at[rows], cs.at[v, b], csend.at[k], crecv.at[k], b2, v))
        mode_copies[-1].start()
    cs[v, b] = sbuf[pl.ds(pl.multiple_of(GROUP * b, GROUP), GROUP)]
    for copy in mode_copies:
        copy.wait_recv()
    gathers = []
    for k in range(1, GROUP):
        v2 = vecs[k]
        gathers.append(remote(cs.at[v], cs.at[v], asend.at[k], arecv.at[k], b, v2))
        gathers[-1].start()
    for copy in gathers:
        copy.wait_recv()

    product = 0.0
    parts = []
    for r in range(GROUP):
        part = cs[:, :, r].reshape(NUM, 6 * KMAX)
        parts.append(part)
        tiled = jnp.concatenate([part] * 8, axis=0)
        product = product + lax.dot_general(
            part, tiled, (((1,), (1,)), ((), ())), precision=HIGHEST,
            preferred_element_type=jnp.float32,
        )
    product = jnp.where(diagonal, product, 0.0)
    gsend[0:1, :] = jnp.sum(product[:8], axis=0, keepdims=True)
    gsend[1:2, :] = jnp.sum(product[8:], axis=0, keepdims=True)
    gram_copies = []
    for k in range(1, GROUP):
        b2 = bands[k]
        gram_copies.append(remote(gsend, gbuf.at[b], msend.at[k], mrecv.at[k], b2, v))
        gram_copies[-1].start()
    gbuf[b] = gsend[...]
    for copy in gram_copies:
        copy.wait_recv()
    gram = (gbuf[0] + gbuf[1]) + (gbuf[2] + gbuf[3])
    gram = gram * (1.0 / size)
    spread = jnp.concatenate(
        [jnp.broadcast_to(gram[i : i + 1], (8, 128)) for i in range(2)], axis=0
    )
    spread = jnp.where(diagonal, spread, 0.0)
    grid = dot_full(permute[:, :NUM], dot_full(spread, unpack))
    grid = jnp.where(lane < NUM, permute, grid)
    for s in range(NUM - 1):
        col = grid[:, NUM + s : NUM + s + 1]
        factor = col / grid[s : s + 1, NUM + s : NUM + s + 1]
        grid = grid - jnp.where(row > s, factor * grid[s : s + 1, :], 0.0)
    pivot = jnp.sum(jnp.where(lane == row + NUM, grid, 0.0), axis=1, keepdims=True)
    root = jnp.sqrt(pivot)
    logs = jnp.broadcast_to(jnp.log(root), (NUM, 128))
    mix = jnp.where(lane < NUM, grid / root, logs)
    mix = dot_full(own_rows[:, :NUM], mix)
    mix_ref[...] = mix

    for r in range(GROUP):
        fresh = dot_full(mix[:, :NUM], parts[r])
        for i in range(GROUP):
            for f in range(3):
                at = 12 * i + GROUP * f + r
                nb[at : at + 1, :] = fresh[i : i + 1, 2 * KMAX * f : 2 * KMAX * (f + 1)]
    for copy in flow_copies + vec_copies + forwards + mode_copies + gathers + gram_copies:
        copy.wait_send()


def final_kernel(nb, mix_ref, inv_ref, out_ref, growth_ref):
    result = dot_split(nb[...], inv_ref)
    for i in range(GROUP):
        growth_ref[i] = mix_ref[i, NUM]
        for f in range(3):
            at = 12 * i + GROUP * f
            out_ref[i, f] = result[at : at + GROUP]


def on_group(vectors, flow, band_cut, order):
    nlon = vectors.shape[3]
    width = -(-nlon // 128) * 128
    inv, fwd = split_table(nlon, KMAX, width)
    any_spec = pl.BlockSpec(memory_space=pltpu.HBM)
    smem = pl.BlockSpec(memory_space=pltpu.SMEM)
    vmem = pl.BlockSpec(memory_space=pltpu.VMEM)
    dma = pltpu.SemaphoreType.DMA
    size = float(3 * NUM * nlon)
    fresh, mix = pl.pallas_call(
        functools.partial(whole_kernel, nlon, width, size),
        out_shape=[
            jax.ShapeDtypeStruct((3 * NUM, 2 * KMAX), jnp.float32),
            jax.ShapeDtypeStruct((8, 128), jnp.float32),
        ],
        in_specs=[any_spec] * 5,
        out_specs=[vmem, vmem],
        scratch_shapes=[
            pltpu.SMEM((GROUP,), jnp.int32),
            pltpu.SMEM((NUM,), jnp.int32),
            pltpu.VMEM((GROUP, 3, GROUP, nlon), jnp.float32),
            pltpu.VMEM((GROUP, GROUP, GROUP, nlon), jnp.float32),
            pltpu.VMEM(fwd.shape, jnp.bfloat16),
            pltpu.VMEM((3, NUM, width), jnp.float32),
            pltpu.VMEM((GROUP, NUM, width), jnp.float32),
            pltpu.VMEM((NUM, 1, 6 * KMAX), jnp.float32),
            pltpu.VMEM((GROUP, GROUP, GROUP, 1, 6 * KMAX), jnp.float32),
            pltpu.VMEM((2, 128), jnp.float32),
            pltpu.VMEM((GROUP, 2, 128), jnp.float32),
            dma((5,)),
        ] + [dma((GROUP,))] * 12,
        compiler_params=pltpu.CompilerParams(
            collective_id=0, has_side_effects=True, vmem_limit_bytes=24 << 20
        ),
        cost_estimate=pl.CostEstimate(flops=10**9, bytes_accessed=10**8, transcendentals=0),
    )(*[pltpu.with_memory_space_constraint(a, pltpu.HBM) for a in (order, band_cut, vectors, flow, jnp.asarray(fwd))])
    return tuple(pl.pallas_call(
        final_kernel,
        out_shape=[
            jax.ShapeDtypeStruct(vectors.shape, jnp.float32),
            jax.ShapeDtypeStruct((GROUP,), jnp.float32),
        ],
        in_specs=[vmem] * 3,
        out_specs=[vmem, smem],
        compiler_params=pltpu.CompilerParams(vmem_limit_bytes=24 << 20),
    )(fresh, mix, jnp.asarray(inv)))


def solution(mesh):
    in_specs = (P(("member", "vec"), None, "band", None), P(None, "band", None), P(), P())
    out_specs = (P(("member", "vec"), None, "band", None), P(("member", "vec")))

    def body(vectors, flow, band_cut, order):
        rows = mesh.shape["band"] * vectors.shape[2]
        square = (mesh.shape["band"], mesh.shape["vec"], vectors.shape[0], vectors.shape[2])
        if rows == band_cut.shape[0] and square == (GROUP,) * 4:
            return on_group(vectors, flow, band_cut, order)
        return on_device(vectors, flow, band_cut, order)

    return jax.shard_map(
        body, mesh=mesh, in_specs=in_specs, out_specs=out_specs, check_vma=False
    )
```

```python
import math

import functools

import jax
import jax.numpy as jnp
import ml_dtypes
import numpy as np
from jax import lax
from jax.experimental import pallas as pl
from jax.experimental.pallas import tpu as pltpu
from jax.sharding import PartitionSpec as P

KMAX = 128
CAP_DEV = 2


step_dt = 0.4
half_dt = 0.2
sixth_dt = 0.4 / 6.0


def extended(block, sides, width):
    for axis, dim in sides:
        count = lax.axis_size(axis)
        forward = [(i, i + 1) for i in range(count - 1)]
        backward = [(target, source) for source, target in forward]
        low = lax.ppermute(
            lax.slice_in_dim(block, block.shape[dim] - width, None, axis=dim), axis, forward
        )
        high = lax.ppermute(lax.slice_in_dim(block, 0, width, axis=dim), axis, backward)
        block = jnp.concatenate([low, block, high], axis=dim)
    return block


def broadcast(value, axis, source):
    kept = jnp.where(lax.axis_index(axis) == source, value, 0).astype(value.dtype)
    return lax.psum(kept, axis)


def tendency(z, coef):
    inner = z[:, :, 1:-1]
    dx = 0.5 * (jnp.roll(inner, -1, 3) - jnp.roll(inner, 1, 3))
    dy = 0.5 * (z[:, :, 2:] - z[:, :, :-2])
    speed_x = coef[0]
    speed_y = coef[1]
    depth = 1.0 + 0.5 * coef[2]
    rotation = 0.5 * coef[3]
    advect = -(speed_x * dx + speed_y * dy)
    t_height = advect[:, 0] - depth * (dx[:, 1] + dy[:, 2])
    t_zonal = advect[:, 1] - dx[:, 0] + rotation * inner[:, 2]
    t_merid = advect[:, 2] - dy[:, 0] - rotation * inner[:, 1]
    return jnp.stack([t_height, t_zonal, t_merid], 1)


def with_rows(state):
    return extended(state, (("band", 2),), 1)


def step_near(state, flow):
    k_one = tendency(with_rows(state), flow)
    k_two = tendency(with_rows(state + half_dt * k_one), flow)
    k_three = tendency(with_rows(state + half_dt * k_two), flow)
    k_four = tendency(with_rows(state + step_dt * k_three), flow)
    return state + sixth_dt * (k_one + 2.0 * k_two + 2.0 * k_three + k_four)


def mode_table(nlon, kmax):
    points = jnp.arange(nlon, dtype=jnp.int32)
    waves = jnp.arange(kmax, dtype=jnp.int32)
    phase = (waves[:, None] * points[None, :] % nlon).astype(jnp.float32) * (2.0 * math.pi / nlon)
    scale = jnp.where(waves == 0, math.sqrt(1.0 / nlon), math.sqrt(2.0 / nlon)).astype(jnp.float32)
    cosines = jnp.cos(phase) * scale[:, None]
    sines = jnp.sin(phase) * math.sqrt(2.0 / nlon)
    return jnp.concatenate([cosines, sines], 0)


def project(rows, cutoff, table, kmax):
    waves = jnp.arange(kmax, dtype=jnp.int32)
    wave_both = jnp.concatenate([waves, waves], 0)
    keep = (wave_both <= cutoff[..., None]).astype(jnp.float32)
    coeffs = jnp.einsum("...l,kl->...k", rows, table, precision=lax.Precision.HIGHEST)
    return jnp.einsum("...k,kl->...l", coeffs * keep, table, precision=lax.Precision.HIGHEST)


def polar_filter(state, band_cut, table):
    nband = lax.axis_size("band")
    me_band = lax.axis_index("band")
    lat_dev = state.shape[2]
    cap_rows = CAP_DEV * lat_dev
    north = me_band < CAP_DEV
    south = me_band >= nband - CAP_DEV
    start = jnp.where(north, me_band * lat_dev, cap_rows + (me_band - nband + CAP_DEV) * lat_dev)
    start = jnp.clip(start, 0, 2 * cap_rows - lat_dev)
    cutoff = lax.dynamic_slice_in_dim(band_cut, start, lat_dev)
    return lax.cond(
        north | south, lambda value: project(value, cutoff, table, KMAX), lambda value: value, state
    )


def on_device(vectors, flow, band_cut, order):
    state = vectors
    nband = lax.axis_size("band")
    lat_dev = state.shape[2]
    table = mode_table(state.shape[3], KMAX)
    for inner_step in range(2):
        state = step_near(state, flow)
    state = polar_filter(state, band_cut, table)
    nblocks = lax.axis_size("vec")
    me_vec = lax.axis_index("vec")
    vec_dev = state.shape[0]
    total = float(3 * nband * lat_dev * state.shape[3])
    flat = state.reshape(vec_dev, -1)
    numbers = jnp.arange(nblocks, dtype=jnp.int32)
    position = jnp.sum(jnp.where(order == me_vec, numbers, 0))
    growth = jnp.zeros((vec_dev,), jnp.float32)
    for turn in range(nblocks):
        panel = broadcast(flat, "vec", order[turn])
        gram = lax.psum(jnp.dot(panel, panel.T, precision=lax.Precision.HIGHEST), "band") / total
        lower = jnp.linalg.cholesky(gram)
        ortho = jax.scipy.linalg.solve_triangular(lower, panel, lower=True)
        coef = lax.psum(jnp.dot(flat, ortho.T, precision=lax.Precision.HIGHEST), "band") / total
        update = flat - jnp.dot(coef, ortho, precision=lax.Precision.HIGHEST)
        flat = jnp.where(position > turn, update, jnp.where(position == turn, ortho, flat))
        growth = jnp.where(position == turn, jnp.log(jnp.diagonal(lower)), growth)
    return (flat.reshape(state.shape), growth)


MESH = pl.DeviceIdType.MESH
HIGHEST = lax.Precision.HIGHEST
GROUP = 4
NUM = GROUP * GROUP


def split_table(nlon, kmax, width):
    waves = np.arange(kmax)[:, None]
    phase = (waves * np.arange(nlon)[None, :] % nlon) * (2.0 * np.pi / nlon)
    scale = np.where(waves == 0, np.sqrt(1.0 / nlon), np.sqrt(2.0 / nlon))
    table = np.concatenate([np.cos(phase) * scale, np.sin(phase) * np.sqrt(2.0 / nlon)], 0)
    table = table.astype(np.float32)
    high = table.astype(ml_dtypes.bfloat16)
    low = (table - high.astype(np.float32)).astype(ml_dtypes.bfloat16)
    rows = ((0, width - nlon), (0, 0))
    return np.stack([high, low]), np.stack([np.pad(high.T, rows), np.pad(low.T, rows)])


def halves(value):
    high = value.astype(jnp.bfloat16)
    return high, (value - high.astype(jnp.float32)).astype(jnp.bfloat16)


def dot_split(value, table_ref):
    high, low = halves(value)
    dot = functools.partial(jnp.dot, preferred_element_type=jnp.float32)
    return dot(high, table_ref[0]) + (dot(low, table_ref[0]) + dot(high, table_ref[1]))


def dot_full(left, right):
    return jnp.dot(left, right, precision=HIGHEST, preferred_element_type=jnp.float32)


def iota(shape, dim):
    return lax.broadcasted_iota(jnp.int32, shape, dim)


def tend_rows(h, u, v, coef):
    neg_u, neg_v, neg_h, rot = coef
    rows, width = h.shape
    row = iota((rows, width), 0)

    def along_x(z):
        return pltpu.roll(z, width - 1, 1) - pltpu.roll(z, 1, 1)

    def along_y(z):
        above = jnp.where(row == rows - 1, 0.0, pltpu.roll(z, rows - 1, 0))
        below = jnp.where(row == 0, 0.0, pltpu.roll(z, 1, 0))
        return above - below

    xh, xu, xv = along_x(h), along_x(u), along_x(v)
    yh, yu, yv = along_y(h), along_y(u), along_y(v)
    th = neg_u * xh + neg_v * yh + neg_h * (xu + yv)
    tu = neg_u * xu + neg_v * yu - 0.5 * xh + rot * v
    tv = neg_u * xv + neg_v * yv - 0.5 * yh - rot * u
    return th, tu, tv


def step_rows(x, coef):
    k = tend_rows(*x, coef)
    total = k
    for scale, weight in ((half_dt, 2.0), (half_dt, 2.0), (step_dt, 1.0)):
        k = tend_rows(*[a + scale * b for a, b in zip(x, k)], coef)
        total = [a + weight * b for a, b in zip(total, k)]
    return [a + sixth_dt * b for a, b in zip(x, total)]


def whole_kernel(
    nlon, width, size,
    order_hbm, cut_hbm, vec_hbm, flow_hbm, fwd_hbm,
    nb, mix_ref,
    order_ref, cut_ref, vbuf, fbuf, fwd, xs, fs, sbuf, cs, gsend, gbuf,
    local_sem, vsend, vrecv, fsend, frecv, gosend, gorecv, csend, crecv, asend, arecv, msend, mrecv,
):
    b = lax.axis_index("band")
    v = lax.axis_index("vec")

    def remote(src, dst, send, recv, b2, v2):
        return pltpu.make_async_remote_copy(
            src_ref=src, dst_ref=dst, send_sem=send, recv_sem=recv,
            device_id={"band": b2, "vec": v2}, device_id_type=MESH,
        )

    own = [
        pltpu.make_async_copy(flow_hbm.at[v], fbuf.at[v, b], local_sem.at[0]),
        pltpu.make_async_copy(vec_hbm.at[b], vbuf.at[b], local_sem.at[1]),
        pltpu.make_async_copy(fwd_hbm, fwd, local_sem.at[2]),
        pltpu.make_async_copy(order_hbm, order_ref, local_sem.at[3]),
        pltpu.make_async_copy(cut_hbm, cut_ref, local_sem.at[4]),
    ]
    for copy in own:
        copy.start()

    barrier = pltpu.get_barrier_semaphore()
    bands = [lax.rem(b + k, GROUP) for k in range(GROUP)]
    vecs = [lax.rem(v + k, GROUP) for k in range(GROUP)]
    for b2, v2 in [(b2, v) for b2 in bands[1:]] + [(b, v2) for v2 in vecs[1:]]:
        pl.semaphore_signal(barrier, inc=1, device_id={"band": b2, "vec": v2}, device_id_type=MESH)
    pl.semaphore_wait(barrier, 2 * GROUP - 2)

    flow_copies, vec_copies = [], []
    for k in range(1, GROUP):
        b2 = bands[k]
        flow_copies.append(
            remote(flow_hbm.at[v], fbuf.at[v, b], fsend.at[k], frecv.at[k], b2, v)
        )
        flow_copies[-1].start()
    for k in range(1, GROUP):
        b2 = bands[k]
        vec_copies.append(remote(vec_hbm.at[b2], vbuf.at[b], vsend.at[k], vrecv.at[k], b2, v))
        vec_copies[-1].start()

    own[3].wait()
    own[4].wait()
    lane = iota((NUM, 128), 1)
    row = iota((NUM, 128), 0)

    def placed(at):
        turn = at // GROUP
        block = jnp.where(
            turn == 0, order_ref[0],
            jnp.where(turn == 1, order_ref[1], jnp.where(turn == 2, order_ref[2], order_ref[3])),
        )
        return GROUP * block + at % GROUP

    permute = (lane == placed(row)).astype(jnp.float32)
    lane_big = iota((128, 128), 1)
    row_big = iota((128, 128), 0)
    unpack = (
        (row_big % NUM == placed(lane_big - NUM)) & (lane_big >= NUM) & (lane_big < 2 * NUM)
    ).astype(jnp.float32)
    diagonal = lane // NUM == row % 8
    own_rows = (placed(lane[:8]) == GROUP * v + row[:8]) & (lane[:8] < NUM) & (row[:8] < GROUP)
    own_rows = own_rows.astype(jnp.float32)
    wave = iota((NUM, 2 * KMAX), 1) % KMAX
    wave_row = iota((NUM, 2 * KMAX), 0)
    cut = jnp.zeros((NUM, 2 * KMAX), jnp.int32)
    for r in range(NUM):
        cut = jnp.where(wave_row == r, cut_ref[r], cut)
    keep = wave <= cut

    own[0].wait()
    for copy in flow_copies:
        copy.wait_recv()
    forwards = []
    for k in range(1, GROUP):
        v2 = vecs[k]
        forwards.append(remote(fbuf.at[v], fbuf.at[v], gosend.at[k], gorecv.at[k], b, v2))
        forwards[-1].start()

    own[1].wait()
    for copy in vec_copies:
        copy.wait_recv()
    for copy in forwards:
        copy.wait_recv()

    extra = width - nlon
    for f in range(3):
        for band in range(GROUP):
            xs[f, GROUP * band : GROUP * (band + 1), :nlon] = vbuf[band, f]
    for f in range(GROUP):
        for band in range(GROUP):
            fs[f, GROUP * band : GROUP * (band + 1), :nlon] = fbuf[f, band]

    def wrapped(z):
        return jnp.concatenate([z, z[:, : extra // 2], z[:, nlon - extra // 2 :]], axis=1)

    x = [wrapped(xs[f, :, :nlon]) for f in range(3)]
    speed_x, speed_y, deep, turning = [wrapped(fs[f, :, :nlon]) for f in range(GROUP)]
    coef = (-0.5 * speed_x, -0.5 * speed_y, -0.5 - 0.25 * deep, 0.5 * turning)
    for _ in range(2):
        x = step_rows(x, coef)

    own[2].wait()
    modes = dot_split(jnp.concatenate(x, axis=0), fwd)
    for f in range(3):
        kept = jnp.where(keep, modes[NUM * f : NUM * (f + 1)], 0.0)
        sbuf[:, 0, 2 * KMAX * f : 2 * KMAX * (f + 1)] = kept

    me = GROUP * v + b
    peers = [(bands[j], vecs[k]) for j in (2, 3, 1, 0) for k in (2, 3, 1, 0)][:-1]
    mode_copies = []
    for k, (b2, v2) in enumerate(peers):
        mode_copies.append(
            remote(sbuf.at[GROUP * b2 + v2], cs.at[v2, me], csend.at[k], crecv.at[k], b2, v2)
        )
        mode_copies[-1].start()
    cs[v, me] = sbuf[GROUP * b + v]
    for copy in mode_copies:
        copy.wait_recv()

    part = cs[v].reshape(NUM, 6 * KMAX)
    tiled = jnp.concatenate([part] * 8, axis=0)
    product = lax.dot_general(
        part, tiled, (((1,), (1,)), ((), ())), precision=HIGHEST,
        preferred_element_type=jnp.float32,
    )
    product = jnp.where(diagonal, product, 0.0)
    gsend[0:1, :] = jnp.sum(product[:8], axis=0, keepdims=True)
    gsend[1:2, :] = jnp.sum(product[8:], axis=0, keepdims=True)
    gram_copies = []
    for k, (b2, v2) in enumerate(peers):
        gram_copies.append(remote(gsend, gbuf.at[me], msend.at[k], mrecv.at[k], b2, v2))
        gram_copies[-1].start()
    gathers = []
    for k in range(1, GROUP):
        v2 = vecs[k]
        gathers.append(remote(cs.at[v], cs.at[v], asend.at[k], arecv.at[k], b, v2))
        gathers[-1].start()
    gbuf[me] = gsend[...]
    for copy in gram_copies:
        copy.wait_recv()
    gram = gbuf[0]
    for k in range(1, NUM):
        gram = gram + gbuf[k]
    gram = gram * (1.0 / size)
    spread = jnp.concatenate(
        [jnp.broadcast_to(gram[i : i + 1], (8, 128)) for i in range(2)], axis=0
    )
    spread = jnp.where(diagonal, spread, 0.0)
    grid = dot_full(permute[:, :NUM], dot_full(spread, unpack))
    grid = jnp.where(lane < NUM, permute, grid)
    for s in range(NUM - 1):
        col = grid[:, NUM + s : NUM + s + 1]
        factor = col / grid[s : s + 1, NUM + s : NUM + s + 1]
        grid = grid - jnp.where(row > s, factor * grid[s : s + 1, :], 0.0)
    pivot = jnp.sum(jnp.where(lane == row + NUM, grid, 0.0), axis=1, keepdims=True)
    root = jnp.sqrt(pivot)
    logs = jnp.broadcast_to(jnp.log(root), (NUM, 128))
    mix = jnp.where(lane < NUM, grid / root, logs)
    mix = dot_full(own_rows[:, :NUM], mix)
    mix_ref[...] = mix

    for copy in gathers:
        copy.wait_recv()
    for r in range(GROUP):
        fresh = dot_full(mix[:, :NUM], cs[r].reshape(NUM, 6 * KMAX))
        for i in range(GROUP):
            for f in range(3):
                at = 12 * i + GROUP * f + r
                nb[at : at + 1, :] = fresh[i : i + 1, 2 * KMAX * f : 2 * KMAX * (f + 1)]
    for copy in flow_copies + vec_copies + forwards + mode_copies + gathers + gram_copies:
        copy.wait_send()


def final_kernel(nb, mix_ref, inv_ref, out_ref, growth_ref):
    result = dot_split(nb[...], inv_ref)
    for i in range(GROUP):
        growth_ref[i] = mix_ref[i, NUM]
        for f in range(3):
            at = 12 * i + GROUP * f
            out_ref[i, f] = result[at : at + GROUP]


def on_group(vectors, flow, band_cut, order):
    nlon = vectors.shape[3]
    width = -(-nlon // 128) * 128
    inv, fwd = split_table(nlon, KMAX, width)
    any_spec = pl.BlockSpec(memory_space=pltpu.HBM)
    smem = pl.BlockSpec(memory_space=pltpu.SMEM)
    vmem = pl.BlockSpec(memory_space=pltpu.VMEM)
    dma = pltpu.SemaphoreType.DMA
    size = float(3 * NUM * nlon)
    fresh, mix = pl.pallas_call(
        functools.partial(whole_kernel, nlon, width, size),
        out_shape=[
            jax.ShapeDtypeStruct((3 * NUM, 2 * KMAX), jnp.float32),
            jax.ShapeDtypeStruct((8, 128), jnp.float32),
        ],
        in_specs=[any_spec] * 5,
        out_specs=[vmem, vmem],
        scratch_shapes=[
            pltpu.SMEM((GROUP,), jnp.int32),
            pltpu.SMEM((NUM,), jnp.int32),
            pltpu.VMEM((GROUP, 3, GROUP, nlon), jnp.float32),
            pltpu.VMEM((GROUP, GROUP, GROUP, nlon), jnp.float32),
            pltpu.VMEM(fwd.shape, jnp.bfloat16),
            pltpu.VMEM((3, NUM, width), jnp.float32),
            pltpu.VMEM((GROUP, NUM, width), jnp.float32),
            pltpu.VMEM((NUM, 1, 6 * KMAX), jnp.float32),
            pltpu.VMEM((GROUP, NUM, 1, 6 * KMAX), jnp.float32),
            pltpu.VMEM((2, 128), jnp.float32),
            pltpu.VMEM((NUM, 2, 128), jnp.float32),
            dma((5,)),
        ] + [dma((GROUP,))] * 6 + [dma((NUM,))] * 2 + [dma((GROUP,))] * 2 + [dma((NUM,))] * 2,
        compiler_params=pltpu.CompilerParams(
            collective_id=0, has_side_effects=True, vmem_limit_bytes=24 << 20
        ),
        cost_estimate=pl.CostEstimate(flops=10**9, bytes_accessed=10**8, transcendentals=0),
    )(*[pltpu.with_memory_space_constraint(a, pltpu.HBM) for a in (order, band_cut, vectors, flow, jnp.asarray(fwd))])
    return tuple(pl.pallas_call(
        final_kernel,
        out_shape=[
            jax.ShapeDtypeStruct(vectors.shape, jnp.float32),
            jax.ShapeDtypeStruct((GROUP,), jnp.float32),
        ],
        in_specs=[vmem] * 3,
        out_specs=[vmem, smem],
        compiler_params=pltpu.CompilerParams(vmem_limit_bytes=24 << 20),
    )(fresh, mix, jnp.asarray(inv)))


def solution(mesh):
    in_specs = (P(("member", "vec"), None, "band", None), P(None, "band", None), P(), P())
    out_specs = (P(("member", "vec"), None, "band", None), P(("member", "vec")))

    def body(vectors, flow, band_cut, order):
        rows = mesh.shape["band"] * vectors.shape[2]
        square = (mesh.shape["band"], mesh.shape["vec"], vectors.shape[0], vectors.shape[2])
        if rows == band_cut.shape[0] and square == (GROUP,) * 4:
            return on_group(vectors, flow, band_cut, order)
        return on_device(vectors, flow, band_cut, order)

    return jax.shard_map(
        body, mesh=mesh, in_specs=in_specs, out_specs=out_specs, check_vma=False
    )
```

```python
import math

import functools

import jax
import jax.numpy as jnp
import ml_dtypes
import numpy as np
from jax import lax
from jax.experimental import pallas as pl
from jax.experimental.pallas import tpu as pltpu
from jax.sharding import PartitionSpec as P

KMAX = 128
CAP_DEV = 2


step_dt = 0.4
half_dt = 0.2
sixth_dt = 0.4 / 6.0


def extended(block, sides, width):
    for axis, dim in sides:
        count = lax.axis_size(axis)
        forward = [(i, i + 1) for i in range(count - 1)]
        backward = [(target, source) for source, target in forward]
        low = lax.ppermute(
            lax.slice_in_dim(block, block.shape[dim] - width, None, axis=dim), axis, forward
        )
        high = lax.ppermute(lax.slice_in_dim(block, 0, width, axis=dim), axis, backward)
        block = jnp.concatenate([low, block, high], axis=dim)
    return block


def broadcast(value, axis, source):
    kept = jnp.where(lax.axis_index(axis) == source, value, 0).astype(value.dtype)
    return lax.psum(kept, axis)


def tendency(z, coef):
    inner = z[:, :, 1:-1]
    dx = 0.5 * (jnp.roll(inner, -1, 3) - jnp.roll(inner, 1, 3))
    dy = 0.5 * (z[:, :, 2:] - z[:, :, :-2])
    speed_x = coef[0]
    speed_y = coef[1]
    depth = 1.0 + 0.5 * coef[2]
    rotation = 0.5 * coef[3]
    advect = -(speed_x * dx + speed_y * dy)
    t_height = advect[:, 0] - depth * (dx[:, 1] + dy[:, 2])
    t_zonal = advect[:, 1] - dx[:, 0] + rotation * inner[:, 2]
    t_merid = advect[:, 2] - dy[:, 0] - rotation * inner[:, 1]
    return jnp.stack([t_height, t_zonal, t_merid], 1)


def with_rows(state):
    return extended(state, (("band", 2),), 1)


def step_near(state, flow):
    k_one = tendency(with_rows(state), flow)
    k_two = tendency(with_rows(state + half_dt * k_one), flow)
    k_three = tendency(with_rows(state + half_dt * k_two), flow)
    k_four = tendency(with_rows(state + step_dt * k_three), flow)
    return state + sixth_dt * (k_one + 2.0 * k_two + 2.0 * k_three + k_four)


def mode_table(nlon, kmax):
    points = jnp.arange(nlon, dtype=jnp.int32)
    waves = jnp.arange(kmax, dtype=jnp.int32)
    phase = (waves[:, None] * points[None, :] % nlon).astype(jnp.float32) * (2.0 * math.pi / nlon)
    scale = jnp.where(waves == 0, math.sqrt(1.0 / nlon), math.sqrt(2.0 / nlon)).astype(jnp.float32)
    cosines = jnp.cos(phase) * scale[:, None]
    sines = jnp.sin(phase) * math.sqrt(2.0 / nlon)
    return jnp.concatenate([cosines, sines], 0)


def project(rows, cutoff, table, kmax):
    waves = jnp.arange(kmax, dtype=jnp.int32)
    wave_both = jnp.concatenate([waves, waves], 0)
    keep = (wave_both <= cutoff[..., None]).astype(jnp.float32)
    coeffs = jnp.einsum("...l,kl->...k", rows, table, precision=lax.Precision.HIGHEST)
    return jnp.einsum("...k,kl->...l", coeffs * keep, table, precision=lax.Precision.HIGHEST)


def polar_filter(state, band_cut, table):
    nband = lax.axis_size("band")
    me_band = lax.axis_index("band")
    lat_dev = state.shape[2]
    cap_rows = CAP_DEV * lat_dev
    north = me_band < CAP_DEV
    south = me_band >= nband - CAP_DEV
    start = jnp.where(north, me_band * lat_dev, cap_rows + (me_band - nband + CAP_DEV) * lat_dev)
    start = jnp.clip(start, 0, 2 * cap_rows - lat_dev)
    cutoff = lax.dynamic_slice_in_dim(band_cut, start, lat_dev)
    return lax.cond(
        north | south, lambda value: project(value, cutoff, table, KMAX), lambda value: value, state
    )


def on_device(vectors, flow, band_cut, order):
    state = vectors
    nband = lax.axis_size("band")
    lat_dev = state.shape[2]
    table = mode_table(state.shape[3], KMAX)
    for inner_step in range(2):
        state = step_near(state, flow)
    state = polar_filter(state, band_cut, table)
    nblocks = lax.axis_size("vec")
    me_vec = lax.axis_index("vec")
    vec_dev = state.shape[0]
    total = float(3 * nband * lat_dev * state.shape[3])
    flat = state.reshape(vec_dev, -1)
    numbers = jnp.arange(nblocks, dtype=jnp.int32)
    position = jnp.sum(jnp.where(order == me_vec, numbers, 0))
    growth = jnp.zeros((vec_dev,), jnp.float32)
    for turn in range(nblocks):
        panel = broadcast(flat, "vec", order[turn])
        gram = lax.psum(jnp.dot(panel, panel.T, precision=lax.Precision.HIGHEST), "band") / total
        lower = jnp.linalg.cholesky(gram)
        ortho = jax.scipy.linalg.solve_triangular(lower, panel, lower=True)
        coef = lax.psum(jnp.dot(flat, ortho.T, precision=lax.Precision.HIGHEST), "band") / total
        update = flat - jnp.dot(coef, ortho, precision=lax.Precision.HIGHEST)
        flat = jnp.where(position > turn, update, jnp.where(position == turn, ortho, flat))
        growth = jnp.where(position == turn, jnp.log(jnp.diagonal(lower)), growth)
    return (flat.reshape(state.shape), growth)


MESH = pl.DeviceIdType.MESH
HIGHEST = lax.Precision.HIGHEST
GROUP = 4
NUM = GROUP * GROUP


def split_table(nlon, kmax, width):
    waves = np.arange(kmax)[:, None]
    phase = (waves * np.arange(nlon)[None, :] % nlon) * (2.0 * np.pi / nlon)
    scale = np.where(waves == 0, np.sqrt(1.0 / nlon), np.sqrt(2.0 / nlon))
    table = np.concatenate([np.cos(phase) * scale, np.sin(phase) * np.sqrt(2.0 / nlon)], 0)
    table = table.astype(np.float32)
    high = table.astype(ml_dtypes.bfloat16)
    low = (table - high.astype(np.float32)).astype(ml_dtypes.bfloat16)
    rows = ((0, width - nlon), (0, 0))
    return np.stack([high, low]), np.stack([np.pad(high.T, rows), np.pad(low.T, rows)])


def halves(value):
    high = value.astype(jnp.bfloat16)
    return high, (value - high.astype(jnp.float32)).astype(jnp.bfloat16)


def dot_split(value, table_ref):
    high, low = halves(value)
    dot = functools.partial(jnp.dot, preferred_element_type=jnp.float32)
    rows = value.shape[0]
    both = dot(jnp.concatenate([high, low], axis=0), table_ref[0])
    return both[:rows] + (both[rows:] + dot(high, table_ref[1]))


def dot_full(left, right):
    return jnp.dot(left, right, precision=HIGHEST, preferred_element_type=jnp.float32)


def iota(shape, dim):
    return lax.broadcasted_iota(jnp.int32, shape, dim)


def tend_rows(h, u, v, coef):
    neg_u, neg_v, neg_h, rot = coef
    rows, width = h.shape
    row = iota((rows, width), 0)

    def along_x(z):
        return pltpu.roll(z, width - 1, 1) - pltpu.roll(z, 1, 1)

    def along_y(z):
        above = jnp.where(row == rows - 1, 0.0, pltpu.roll(z, rows - 1, 0))
        below = jnp.where(row == 0, 0.0, pltpu.roll(z, 1, 0))
        return above - below

    xh, xu, xv = along_x(h), along_x(u), along_x(v)
    yh, yu, yv = along_y(h), along_y(u), along_y(v)
    th = neg_u * xh + neg_v * yh + neg_h * (xu + yv)
    tu = neg_u * xu + neg_v * yu - 0.5 * xh + rot * v
    tv = neg_u * xv + neg_v * yv - 0.5 * yh - rot * u
    return th, tu, tv


def step_rows(x, coef):
    k = tend_rows(*x, coef)
    total = k
    for scale, weight in ((half_dt, 2.0), (half_dt, 2.0), (step_dt, 1.0)):
        k = tend_rows(*[a + scale * b for a, b in zip(x, k)], coef)
        total = [a + weight * b for a, b in zip(total, k)]
    return [a + sixth_dt * b for a, b in zip(x, total)]


def whole_kernel(
    nlon, width, size,
    order_hbm, cut_hbm, vec_hbm, flow_hbm, fwd_hbm,
    nb, mix_ref,
    order_ref, cut_ref, vbuf, fbuf, fwd, xs, fs, sbuf, cs, gsend, gbuf,
    local_sem, vsend, vrecv, fsend, frecv, gosend, gorecv, csend, crecv, asend, arecv, msend, mrecv,
):
    b = lax.axis_index("band")
    v = lax.axis_index("vec")

    def remote(src, dst, send, recv, b2, v2):
        return pltpu.make_async_remote_copy(
            src_ref=src, dst_ref=dst, send_sem=send, recv_sem=recv,
            device_id={"band": b2, "vec": v2}, device_id_type=MESH,
        )

    own = [
        pltpu.make_async_copy(flow_hbm.at[v], fbuf.at[v, b], local_sem.at[0]),
        pltpu.make_async_copy(vec_hbm.at[b], vbuf.at[b], local_sem.at[1]),
        pltpu.make_async_copy(fwd_hbm, fwd, local_sem.at[2]),
        pltpu.make_async_copy(order_hbm, order_ref, local_sem.at[3]),
        pltpu.make_async_copy(cut_hbm, cut_ref, local_sem.at[4]),
    ]
    for copy in own:
        copy.start()

    barrier = pltpu.get_barrier_semaphore()
    bands = [lax.rem(b + k, GROUP) for k in range(GROUP)]
    vecs = [lax.rem(v + k, GROUP) for k in range(GROUP)]
    for b2, v2 in [(b2, v) for b2 in bands[1:]] + [(b, v2) for v2 in vecs[1:]]:
        pl.semaphore_signal(barrier, inc=1, device_id={"band": b2, "vec": v2}, device_id_type=MESH)
    pl.semaphore_wait(barrier, 2 * GROUP - 2)

    flow_copies, vec_copies = [], []
    for k in range(1, GROUP):
        b2 = bands[k]
        flow_copies.append(
            remote(flow_hbm.at[v], fbuf.at[v, b], fsend.at[k], frecv.at[k], b2, v)
        )
        flow_copies[-1].start()
    for k in range(1, GROUP):
        b2 = bands[k]
        vec_copies.append(remote(vec_hbm.at[b2], vbuf.at[b], vsend.at[k], vrecv.at[k], b2, v))
        vec_copies[-1].start()

    forwards = []

    def forward(j, piece, source):
        for k in (2, 3, 1):
            at = GROUP * j + k
            forwards.append(
                remote(piece, fbuf.at[v, source], gosend.at[at], gorecv.at[at], b, vecs[k])
            )
            forwards[-1].start()

    forward(0, flow_hbm.at[v], b)
    own[3].wait()
    own[4].wait()
    lane = iota((NUM, 128), 1)
    row = iota((NUM, 128), 0)

    def placed(at):
        turn = at // GROUP
        block = jnp.where(
            turn == 0, order_ref[0],
            jnp.where(turn == 1, order_ref[1], jnp.where(turn == 2, order_ref[2], order_ref[3])),
        )
        return GROUP * block + at % GROUP

    permute = (lane == placed(row)).astype(jnp.float32)
    lane_big = iota((128, 128), 1)
    row_big = iota((128, 128), 0)
    unpack = (
        (row_big % NUM == placed(lane_big - NUM)) & (lane_big >= NUM) & (lane_big < 2 * NUM)
    ).astype(jnp.float32)
    diagonal = lane // NUM == row % 8
    own_rows = (placed(lane[:8]) == GROUP * v + row[:8]) & (lane[:8] < NUM) & (row[:8] < GROUP)
    own_rows = own_rows.astype(jnp.float32)
    wave = iota((NUM, 2 * KMAX), 1) % KMAX
    wave_row = iota((NUM, 2 * KMAX), 0)
    cut = jnp.zeros((NUM, 2 * KMAX), jnp.int32)
    for r in range(NUM):
        cut = jnp.where(wave_row == r, cut_ref[r], cut)
    keep = wave <= cut

    own[0].wait()
    for j in (1, 3, 2):
        flow_copies[j - 1].wait_recv()
        source = bands[GROUP - j]
        forward(j, fbuf.at[v, source], source)

    own[1].wait()
    for copy in vec_copies:
        copy.wait_recv()
    for copy in forwards:
        copy.wait_recv()

    extra = width - nlon
    for f in range(3):
        for band in range(GROUP):
            xs[f, GROUP * band : GROUP * (band + 1), :nlon] = vbuf[band, f]
    for f in range(GROUP):
        for band in range(GROUP):
            fs[f, GROUP * band : GROUP * (band + 1), :nlon] = fbuf[f, band]

    def wrapped(z):
        return jnp.concatenate([z, z[:, : extra // 2], z[:, nlon - extra // 2 :]], axis=1)

    x = [wrapped(xs[f, :, :nlon]) for f in range(3)]
    speed_x, speed_y, deep, turning = [wrapped(fs[f, :, :nlon]) for f in range(GROUP)]
    coef = (-0.5 * speed_x, -0.5 * speed_y, -0.5 - 0.25 * deep, 0.5 * turning)
    for _ in range(2):
        x = step_rows(x, coef)

    own[2].wait()
    modes = dot_split(jnp.concatenate(x, axis=0), fwd)
    for f in range(3):
        kept = jnp.where(keep, modes[NUM * f : NUM * (f + 1)], 0.0)
        sbuf[:, 0, 2 * KMAX * f : 2 * KMAX * (f + 1)] = kept

    me = GROUP * v + b
    peers = [(bands[j], vecs[k]) for j in (2, 3, 1, 0) for k in (2, 3, 1, 0)][:-1]
    mode_copies = []
    for k, (b2, v2) in enumerate(peers):
        mode_copies.append(
            remote(sbuf.at[GROUP * b2 + v2], cs.at[v2, me], csend.at[k], crecv.at[k], b2, v2)
        )
        mode_copies[-1].start()
    cs[v, me] = sbuf[GROUP * b + v]
    for copy in mode_copies:
        copy.wait_recv()

    part = cs[v].reshape(NUM, 6 * KMAX)
    tiled = jnp.concatenate([part] * 8, axis=0)
    product = lax.dot_general(
        part, tiled, (((1,), (1,)), ((), ())), precision=HIGHEST,
        preferred_element_type=jnp.float32,
    )
    product = jnp.where(diagonal, product, 0.0)
    gsend[0:1, :] = jnp.sum(product[:8], axis=0, keepdims=True)
    gsend[1:2, :] = jnp.sum(product[8:], axis=0, keepdims=True)
    gram_copies = []
    for k, (b2, v2) in enumerate(peers):
        gram_copies.append(remote(gsend, gbuf.at[me], msend.at[k], mrecv.at[k], b2, v2))
        gram_copies[-1].start()
    gathers = []
    for k in range(1, GROUP):
        v2 = vecs[k]
        gathers.append(remote(cs.at[v], cs.at[v], asend.at[k], arecv.at[k], b, v2))
        gathers[-1].start()
    gbuf[me] = gsend[...]
    for copy in gram_copies:
        copy.wait_recv()
    gram = gbuf[0]
    for k in range(1, NUM):
        gram = gram + gbuf[k]
    gram = gram * (1.0 / size)
    spread = jnp.concatenate(
        [jnp.broadcast_to(gram[i : i + 1], (8, 128)) for i in range(2)], axis=0
    )
    spread = jnp.where(diagonal, spread, 0.0)
    grid = dot_full(permute[:, :NUM], dot_full(spread, unpack))
    grid = jnp.where(lane < NUM, permute, grid)
    for s in range(NUM - 1):
        col = grid[:, NUM + s : NUM + s + 1]
        factor = col / grid[s : s + 1, NUM + s : NUM + s + 1]
        grid = grid - jnp.where(row > s, factor * grid[s : s + 1, :], 0.0)
    pivot = jnp.sum(jnp.where(lane == row + NUM, grid, 0.0), axis=1, keepdims=True)
    root = jnp.sqrt(pivot)
    logs = jnp.broadcast_to(jnp.log(root), (NUM, 128))
    mix = jnp.where(lane < NUM, grid / root, logs)
    mix = dot_full(own_rows[:, :NUM], mix)
    mix_ref[...] = mix

    for copy in gathers:
        copy.wait_recv()
    for r in range(GROUP):
        fresh = dot_full(mix[:, :NUM], cs[r].reshape(NUM, 6 * KMAX))
        for i in range(GROUP):
            for f in range(3):
                at = 12 * i + GROUP * f + r
                nb[at : at + 1, :] = fresh[i : i + 1, 2 * KMAX * f : 2 * KMAX * (f + 1)]
    for copy in flow_copies + vec_copies + forwards + mode_copies + gathers + gram_copies:
        copy.wait_send()


def final_kernel(nb, mix_ref, inv_ref, out_ref, growth_ref):
    result = dot_split(nb[...], inv_ref)
    for i in range(GROUP):
        growth_ref[i] = mix_ref[i, NUM]
        for f in range(3):
            at = 12 * i + GROUP * f
            out_ref[i, f] = result[at : at + GROUP]


def on_group(vectors, flow, band_cut, order):
    nlon = vectors.shape[3]
    width = -(-nlon // 128) * 128
    inv, fwd = split_table(nlon, KMAX, width)
    any_spec = pl.BlockSpec(memory_space=pltpu.HBM)
    smem = pl.BlockSpec(memory_space=pltpu.SMEM)
    vmem = pl.BlockSpec(memory_space=pltpu.VMEM)
    dma = pltpu.SemaphoreType.DMA
    size = float(3 * NUM * nlon)
    fresh, mix = pl.pallas_call(
        functools.partial(whole_kernel, nlon, width, size),
        out_shape=[
            jax.ShapeDtypeStruct((3 * NUM, 2 * KMAX), jnp.float32),
            jax.ShapeDtypeStruct((8, 128), jnp.float32),
        ],
        in_specs=[any_spec] * 5,
        out_specs=[vmem, vmem],
        scratch_shapes=[
            pltpu.SMEM((GROUP,), jnp.int32),
            pltpu.SMEM((NUM,), jnp.int32),
            pltpu.VMEM((GROUP, 3, GROUP, nlon), jnp.float32),
            pltpu.VMEM((GROUP, GROUP, GROUP, nlon), jnp.float32),
            pltpu.VMEM(fwd.shape, jnp.bfloat16),
            pltpu.VMEM((3, NUM, width), jnp.float32),
            pltpu.VMEM((GROUP, NUM, width), jnp.float32),
            pltpu.VMEM((NUM, 1, 6 * KMAX), jnp.float32),
            pltpu.VMEM((GROUP, NUM, 1, 6 * KMAX), jnp.float32),
            pltpu.VMEM((2, 128), jnp.float32),
            pltpu.VMEM((NUM, 2, 128), jnp.float32),
            dma((5,)),
        ] + [dma((GROUP,))] * 4 + [dma((NUM,))] * 4 + [dma((GROUP,))] * 2 + [dma((NUM,))] * 2,
        compiler_params=pltpu.CompilerParams(
            collective_id=0, has_side_effects=True, vmem_limit_bytes=24 << 20
        ),
        cost_estimate=pl.CostEstimate(flops=10**9, bytes_accessed=10**8, transcendentals=0),
    )(*[pltpu.with_memory_space_constraint(a, pltpu.HBM) for a in (order, band_cut, vectors, flow, jnp.asarray(fwd))])
    return tuple(pl.pallas_call(
        final_kernel,
        out_shape=[
            jax.ShapeDtypeStruct(vectors.shape, jnp.float32),
            jax.ShapeDtypeStruct((GROUP,), jnp.float32),
        ],
        in_specs=[vmem] * 3,
        out_specs=[vmem, smem],
        compiler_params=pltpu.CompilerParams(vmem_limit_bytes=24 << 20),
    )(fresh, mix, jnp.asarray(inv)))


def solution(mesh):
    in_specs = (P(("member", "vec"), None, "band", None), P(None, "band", None), P(), P())
    out_specs = (P(("member", "vec"), None, "band", None), P(("member", "vec")))

    def body(vectors, flow, band_cut, order):
        rows = mesh.shape["band"] * vectors.shape[2]
        square = (mesh.shape["band"], mesh.shape["vec"], vectors.shape[0], vectors.shape[2])
        if rows == band_cut.shape[0] and square == (GROUP,) * 4:
            return on_group(vectors, flow, band_cut, order)
        return on_device(vectors, flow, band_cut, order)

    return jax.shard_map(
        body, mesh=mesh, in_specs=in_specs, out_specs=out_specs, check_vma=False
    )
```

```python
import math

import functools

import jax
import jax.numpy as jnp
import ml_dtypes
import numpy as np
from jax import lax
from jax.experimental import pallas as pl
from jax.experimental.pallas import tpu as pltpu
from jax.sharding import PartitionSpec as P

KMAX = 128
CAP_DEV = 2


step_dt = 0.4
half_dt = 0.2
sixth_dt = 0.4 / 6.0


def extended(block, sides, width):
    for axis, dim in sides:
        count = lax.axis_size(axis)
        forward = [(i, i + 1) for i in range(count - 1)]
        backward = [(target, source) for source, target in forward]
        low = lax.ppermute(
            lax.slice_in_dim(block, block.shape[dim] - width, None, axis=dim), axis, forward
        )
        high = lax.ppermute(lax.slice_in_dim(block, 0, width, axis=dim), axis, backward)
        block = jnp.concatenate([low, block, high], axis=dim)
    return block


def broadcast(value, axis, source):
    kept = jnp.where(lax.axis_index(axis) == source, value, 0).astype(value.dtype)
    return lax.psum(kept, axis)


def tendency(z, coef):
    inner = z[:, :, 1:-1]
    dx = 0.5 * (jnp.roll(inner, -1, 3) - jnp.roll(inner, 1, 3))
    dy = 0.5 * (z[:, :, 2:] - z[:, :, :-2])
    speed_x = coef[0]
    speed_y = coef[1]
    depth = 1.0 + 0.5 * coef[2]
    rotation = 0.5 * coef[3]
    advect = -(speed_x * dx + speed_y * dy)
    t_height = advect[:, 0] - depth * (dx[:, 1] + dy[:, 2])
    t_zonal = advect[:, 1] - dx[:, 0] + rotation * inner[:, 2]
    t_merid = advect[:, 2] - dy[:, 0] - rotation * inner[:, 1]
    return jnp.stack([t_height, t_zonal, t_merid], 1)


def with_rows(state):
    return extended(state, (("band", 2),), 1)


def step_near(state, flow):
    k_one = tendency(with_rows(state), flow)
    k_two = tendency(with_rows(state + half_dt * k_one), flow)
    k_three = tendency(with_rows(state + half_dt * k_two), flow)
    k_four = tendency(with_rows(state + step_dt * k_three), flow)
    return state + sixth_dt * (k_one + 2.0 * k_two + 2.0 * k_three + k_four)


def mode_table(nlon, kmax):
    points = jnp.arange(nlon, dtype=jnp.int32)
    waves = jnp.arange(kmax, dtype=jnp.int32)
    phase = (waves[:, None] * points[None, :] % nlon).astype(jnp.float32) * (2.0 * math.pi / nlon)
    scale = jnp.where(waves == 0, math.sqrt(1.0 / nlon), math.sqrt(2.0 / nlon)).astype(jnp.float32)
    cosines = jnp.cos(phase) * scale[:, None]
    sines = jnp.sin(phase) * math.sqrt(2.0 / nlon)
    return jnp.concatenate([cosines, sines], 0)


def project(rows, cutoff, table, kmax):
    waves = jnp.arange(kmax, dtype=jnp.int32)
    wave_both = jnp.concatenate([waves, waves], 0)
    keep = (wave_both <= cutoff[..., None]).astype(jnp.float32)
    coeffs = jnp.einsum("...l,kl->...k", rows, table, precision=lax.Precision.HIGHEST)
    return jnp.einsum("...k,kl->...l", coeffs * keep, table, precision=lax.Precision.HIGHEST)


def polar_filter(state, band_cut, table):
    nband = lax.axis_size("band")
    me_band = lax.axis_index("band")
    lat_dev = state.shape[2]
    cap_rows = CAP_DEV * lat_dev
    north = me_band < CAP_DEV
    south = me_band >= nband - CAP_DEV
    start = jnp.where(north, me_band * lat_dev, cap_rows + (me_band - nband + CAP_DEV) * lat_dev)
    start = jnp.clip(start, 0, 2 * cap_rows - lat_dev)
    cutoff = lax.dynamic_slice_in_dim(band_cut, start, lat_dev)
    return lax.cond(
        north | south, lambda value: project(value, cutoff, table, KMAX), lambda value: value, state
    )


def on_device(vectors, flow, band_cut, order):
    state = vectors
    nband = lax.axis_size("band")
    lat_dev = state.shape[2]
    table = mode_table(state.shape[3], KMAX)
    for inner_step in range(2):
        state = step_near(state, flow)
    state = polar_filter(state, band_cut, table)
    nblocks = lax.axis_size("vec")
    me_vec = lax.axis_index("vec")
    vec_dev = state.shape[0]
    total = float(3 * nband * lat_dev * state.shape[3])
    flat = state.reshape(vec_dev, -1)
    numbers = jnp.arange(nblocks, dtype=jnp.int32)
    position = jnp.sum(jnp.where(order == me_vec, numbers, 0))
    growth = jnp.zeros((vec_dev,), jnp.float32)
    for turn in range(nblocks):
        panel = broadcast(flat, "vec", order[turn])
        gram = lax.psum(jnp.dot(panel, panel.T, precision=lax.Precision.HIGHEST), "band") / total
        lower = jnp.linalg.cholesky(gram)
        ortho = jax.scipy.linalg.solve_triangular(lower, panel, lower=True)
        coef = lax.psum(jnp.dot(flat, ortho.T, precision=lax.Precision.HIGHEST), "band") / total
        update = flat - jnp.dot(coef, ortho, precision=lax.Precision.HIGHEST)
        flat = jnp.where(position > turn, update, jnp.where(position == turn, ortho, flat))
        growth = jnp.where(position == turn, jnp.log(jnp.diagonal(lower)), growth)
    return (flat.reshape(state.shape), growth)


MESH = pl.DeviceIdType.MESH
HIGHEST = lax.Precision.HIGHEST
GROUP = 4
NUM = GROUP * GROUP


def split_table(nlon, kmax, width):
    waves = np.arange(kmax)[:, None]
    phase = (waves * np.arange(nlon)[None, :] % nlon) * (2.0 * np.pi / nlon)
    scale = np.where(waves == 0, np.sqrt(1.0 / nlon), np.sqrt(2.0 / nlon))
    table = np.concatenate([np.cos(phase) * scale, np.sin(phase) * np.sqrt(2.0 / nlon)], 0)
    table = table.astype(np.float32)
    high = table.astype(ml_dtypes.bfloat16)
    low = (table - high.astype(np.float32)).astype(ml_dtypes.bfloat16)
    rows = ((0, width - nlon), (0, 0))
    return np.stack([high, low]), np.stack([np.pad(high.T, rows), np.pad(low.T, rows)])


def halves(value):
    high = value.astype(jnp.bfloat16)
    return high, (value - high.astype(jnp.float32)).astype(jnp.bfloat16)


def dot_split(value, table_ref):
    high, low = halves(value)
    dot = functools.partial(jnp.dot, preferred_element_type=jnp.float32)
    rows = value.shape[0]
    both = dot(jnp.concatenate([high, low], axis=0), table_ref[0])
    return both[:rows] + (both[rows:] + dot(high, table_ref[1]))


def dot_full(left, right):
    return jnp.dot(left, right, precision=HIGHEST, preferred_element_type=jnp.float32)


def iota(shape, dim):
    return lax.broadcasted_iota(jnp.int32, shape, dim)


def tend_rows(h, u, v, coef):
    neg_u, neg_v, neg_h, rot = coef
    rows, width = h.shape
    row = iota((rows, width), 0)

    def along_x(z):
        return pltpu.roll(z, width - 1, 1) - pltpu.roll(z, 1, 1)

    def along_y(z):
        above = jnp.where(row == rows - 1, 0.0, pltpu.roll(z, rows - 1, 0))
        below = jnp.where(row == 0, 0.0, pltpu.roll(z, 1, 0))
        return above - below

    xh, xu, xv = along_x(h), along_x(u), along_x(v)
    yh, yu, yv = along_y(h), along_y(u), along_y(v)
    th = neg_u * xh + neg_v * yh + neg_h * (xu + yv)
    tu = neg_u * xu + neg_v * yu - 0.5 * xh + rot * v
    tv = neg_u * xv + neg_v * yv - 0.5 * yh - rot * u
    return th, tu, tv


def step_rows(x, coef):
    k = tend_rows(*x, coef)
    total = k
    for scale, weight in ((half_dt, 2.0), (half_dt, 2.0), (step_dt, 1.0)):
        k = tend_rows(*[a + scale * b for a, b in zip(x, k)], coef)
        total = [a + weight * b for a, b in zip(total, k)]
    return [a + sixth_dt * b for a, b in zip(x, total)]


def whole_kernel(
    nlon, width, size,
    order_hbm, cut_hbm, vec_hbm, flow_hbm, fwd_hbm,
    nb, mix_ref,
    order_ref, cut_ref, vbuf, fbuf, fwd, xs, fs, sbuf, cs, gsend, gbuf,
    local_sem, vsend, vrecv, fsend, frecv, gosend, gorecv, csend, crecv, asend, arecv, msend, mrecv,
):
    b = lax.axis_index("band")
    v = lax.axis_index("vec")

    def remote(src, dst, send, recv, b2, v2):
        return pltpu.make_async_remote_copy(
            src_ref=src, dst_ref=dst, send_sem=send, recv_sem=recv,
            device_id={"band": b2, "vec": v2}, device_id_type=MESH,
        )

    own = [
        pltpu.make_async_copy(flow_hbm.at[v], fbuf.at[v, b], local_sem.at[0]),
        pltpu.make_async_copy(vec_hbm.at[b], vbuf.at[b], local_sem.at[1]),
        pltpu.make_async_copy(fwd_hbm, fwd, local_sem.at[2]),
        pltpu.make_async_copy(order_hbm, order_ref, local_sem.at[3]),
        pltpu.make_async_copy(cut_hbm, cut_ref, local_sem.at[4]),
    ]
    for copy in own:
        copy.start()

    barrier = pltpu.get_barrier_semaphore()
    bands = [lax.rem(b + k, GROUP) for k in range(GROUP)]
    vecs = [lax.rem(v + k, GROUP) for k in range(GROUP)]
    for b2, v2 in [(b2, v) for b2 in bands[1:]] + [(b, v2) for v2 in vecs[1:]]:
        pl.semaphore_signal(barrier, inc=1, device_id={"band": b2, "vec": v2}, device_id_type=MESH)
    pl.semaphore_wait(barrier, 2 * GROUP - 2)

    flow_copies, vec_copies = [], []
    for k in range(1, GROUP):
        b2 = bands[k]
        flow_copies.append(
            remote(flow_hbm.at[v], fbuf.at[v, b], fsend.at[k], frecv.at[k], b2, v)
        )
        flow_copies[-1].start()
    forwards = []

    def forward(j, piece, source):
        for k in (2, 3, 1):
            at = GROUP * j + k
            forwards.append(
                remote(piece, fbuf.at[v, source], gosend.at[at], gorecv.at[at], b, vecs[k])
            )
            forwards[-1].start()

    forward(0, flow_hbm.at[v], b)

    for k in range(1, GROUP):
        b2 = bands[k]
        vec_copies.append(remote(vec_hbm.at[b2], vbuf.at[b], vsend.at[k], vrecv.at[k], b2, v))
        vec_copies[-1].start()

    own[3].wait()
    own[4].wait()
    lane = iota((NUM, 128), 1)
    row = iota((NUM, 128), 0)

    def placed(at):
        turn = at // GROUP
        block = jnp.where(
            turn == 0, order_ref[0],
            jnp.where(turn == 1, order_ref[1], jnp.where(turn == 2, order_ref[2], order_ref[3])),
        )
        return GROUP * block + at % GROUP

    permute = (lane == placed(row)).astype(jnp.float32)
    lane_big = iota((128, 128), 1)
    row_big = iota((128, 128), 0)
    unpack = (
        (row_big % NUM == placed(lane_big - NUM)) & (lane_big >= NUM) & (lane_big < 2 * NUM)
    ).astype(jnp.float32)
    diagonal = lane // NUM == row % 8
    own_rows = (placed(lane[:8]) == GROUP * v + row[:8]) & (lane[:8] < NUM) & (row[:8] < GROUP)
    own_rows = own_rows.astype(jnp.float32)
    wave = iota((NUM, 2 * KMAX), 1) % KMAX
    wave_row = iota((NUM, 2 * KMAX), 0)
    cut = jnp.zeros((NUM, 2 * KMAX), jnp.int32)
    for r in range(NUM):
        cut = jnp.where(wave_row == r, cut_ref[r], cut)
    keep = wave <= cut

    own[0].wait()
    for j in (1, 3, 2):
        flow_copies[j - 1].wait_recv()
        source = bands[GROUP - j]
        forward(j, fbuf.at[v, source], source)

    own[1].wait()
    for copy in vec_copies:
        copy.wait_recv()
    for copy in forwards:
        copy.wait_recv()

    extra = width - nlon
    for f in range(3):
        for band in range(GROUP):
            xs[f, GROUP * band : GROUP * (band + 1), :nlon] = vbuf[band, f]
    for f in range(GROUP):
        for band in range(GROUP):
            fs[f, GROUP * band : GROUP * (band + 1), :nlon] = fbuf[f, band]

    def wrapped(z):
        return jnp.concatenate([z, z[:, : extra // 2], z[:, nlon - extra // 2 :]], axis=1)

    x = [wrapped(xs[f, :, :nlon]) for f in range(3)]
    speed_x, speed_y, deep, turning = [wrapped(fs[f, :, :nlon]) for f in range(GROUP)]
    coef = (-0.5 * speed_x, -0.5 * speed_y, -0.5 - 0.25 * deep, 0.5 * turning)
    for _ in range(2):
        x = step_rows(x, coef)

    own[2].wait()
    modes = dot_split(jnp.concatenate(x, axis=0), fwd)
    for f in range(3):
        kept = jnp.where(keep, modes[NUM * f : NUM * (f + 1)], 0.0)
        sbuf[:, 0, 2 * KMAX * f : 2 * KMAX * (f + 1)] = kept

    me = GROUP * v + b
    peers = [(bands[j], vecs[k]) for j in (2, 3, 1, 0) for k in (2, 3, 1, 0)][:-1]
    mode_copies = []
    for k, (b2, v2) in enumerate(peers):
        mode_copies.append(
            remote(sbuf.at[GROUP * b2 + v2], cs.at[v2, me], csend.at[k], crecv.at[k], b2, v2)
        )
        mode_copies[-1].start()
    cs[v, me] = sbuf[GROUP * b + v]
    for copy in mode_copies:
        copy.wait_recv()

    part = cs[v].reshape(NUM, 6 * KMAX)
    tiled = jnp.concatenate([part] * 8, axis=0)
    product = lax.dot_general(
        part, tiled, (((1,), (1,)), ((), ())), precision=HIGHEST,
        preferred_element_type=jnp.float32,
    )
    product = jnp.where(diagonal, product, 0.0)
    gsend[0:1, :] = jnp.sum(product[:8], axis=0, keepdims=True)
    gsend[1:2, :] = jnp.sum(product[8:], axis=0, keepdims=True)
    gram_copies = []
    for k, (b2, v2) in enumerate(peers):
        gram_copies.append(remote(gsend, gbuf.at[me], msend.at[k], mrecv.at[k], b2, v2))
        gram_copies[-1].start()
    gathers = []
    for k in range(1, GROUP):
        v2 = vecs[k]
        gathers.append(remote(cs.at[v], cs.at[v], asend.at[k], arecv.at[k], b, v2))
        gathers[-1].start()
    gbuf[me] = gsend[...]
    for copy in gram_copies:
        copy.wait_recv()
    gram = gbuf[0]
    for k in range(1, NUM):
        gram = gram + gbuf[k]
    gram = gram * (1.0 / size)
    spread = jnp.concatenate(
        [jnp.broadcast_to(gram[i : i + 1], (8, 128)) for i in range(2)], axis=0
    )
    spread = jnp.where(diagonal, spread, 0.0)
    grid = dot_full(permute[:, :NUM], dot_full(spread, unpack))
    grid = jnp.where(lane < NUM, permute, grid)
    for s in range(NUM - 1):
        col = grid[:, NUM + s : NUM + s + 1]
        factor = col / grid[s : s + 1, NUM + s : NUM + s + 1]
        grid = grid - jnp.where(row > s, factor * grid[s : s + 1, :], 0.0)
    pivot = jnp.sum(jnp.where(lane == row + NUM, grid, 0.0), axis=1, keepdims=True)
    root = jnp.sqrt(pivot)
    logs = jnp.broadcast_to(jnp.log(root), (NUM, 128))
    mix = jnp.where(lane < NUM, grid / root, logs)
    mix = dot_full(own_rows[:, :NUM], mix)
    mix_ref[...] = mix

    for copy in gathers:
        copy.wait_recv()
    for r in range(GROUP):
        fresh = dot_full(mix[:, :NUM], cs[r].reshape(NUM, 6 * KMAX))
        for i in range(GROUP):
            for f in range(3):
                at = 12 * i + GROUP * f + r
                nb[at : at + 1, :] = fresh[i : i + 1, 2 * KMAX * f : 2 * KMAX * (f + 1)]
    for copy in flow_copies + vec_copies + forwards + mode_copies + gathers + gram_copies:
        copy.wait_send()


def final_kernel(nb, mix_ref, inv_ref, out_ref, growth_ref):
    result = dot_split(nb[...], inv_ref)
    for i in range(GROUP):
        growth_ref[i] = mix_ref[i, NUM]
        for f in range(3):
            at = 12 * i + GROUP * f
            out_ref[i, f] = result[at : at + GROUP]


def on_group(vectors, flow, band_cut, order):
    nlon = vectors.shape[3]
    width = -(-nlon // 128) * 128
    inv, fwd = split_table(nlon, KMAX, width)
    any_spec = pl.BlockSpec(memory_space=pltpu.HBM)
    smem = pl.BlockSpec(memory_space=pltpu.SMEM)
    vmem = pl.BlockSpec(memory_space=pltpu.VMEM)
    dma = pltpu.SemaphoreType.DMA
    size = float(3 * NUM * nlon)
    fresh, mix = pl.pallas_call(
        functools.partial(whole_kernel, nlon, width, size),
        out_shape=[
            jax.ShapeDtypeStruct((3 * NUM, 2 * KMAX), jnp.float32),
            jax.ShapeDtypeStruct((8, 128), jnp.float32),
        ],
        in_specs=[any_spec] * 5,
        out_specs=[vmem, vmem],
        scratch_shapes=[
            pltpu.SMEM((GROUP,), jnp.int32),
            pltpu.SMEM((NUM,), jnp.int32),
            pltpu.VMEM((GROUP, 3, GROUP, nlon), jnp.float32),
            pltpu.VMEM((GROUP, GROUP, GROUP, nlon), jnp.float32),
            pltpu.VMEM(fwd.shape, jnp.bfloat16),
            pltpu.VMEM((3, NUM, width), jnp.float32),
            pltpu.VMEM((GROUP, NUM, width), jnp.float32),
            pltpu.VMEM((NUM, 1, 6 * KMAX), jnp.float32),
            pltpu.VMEM((GROUP, NUM, 1, 6 * KMAX), jnp.float32),
            pltpu.VMEM((2, 128), jnp.float32),
            pltpu.VMEM((NUM, 2, 128), jnp.float32),
            dma((5,)),
        ] + [dma((GROUP,))] * 4 + [dma((NUM,))] * 4 + [dma((GROUP,))] * 2 + [dma((NUM,))] * 2,
        compiler_params=pltpu.CompilerParams(
            collective_id=0, has_side_effects=True, vmem_limit_bytes=24 << 20
        ),
        cost_estimate=pl.CostEstimate(flops=10**9, bytes_accessed=10**8, transcendentals=0),
    )(*[pltpu.with_memory_space_constraint(a, pltpu.HBM) for a in (order, band_cut, vectors, flow, jnp.asarray(fwd))])
    return tuple(pl.pallas_call(
        final_kernel,
        out_shape=[
            jax.ShapeDtypeStruct(vectors.shape, jnp.float32),
            jax.ShapeDtypeStruct((GROUP,), jnp.float32),
        ],
        in_specs=[vmem] * 3,
        out_specs=[vmem, smem],
        compiler_params=pltpu.CompilerParams(vmem_limit_bytes=24 << 20),
    )(fresh, mix, jnp.asarray(inv)))


def solution(mesh):
    in_specs = (P(("member", "vec"), None, "band", None), P(None, "band", None), P(), P())
    out_specs = (P(("member", "vec"), None, "band", None), P(("member", "vec")))

    def body(vectors, flow, band_cut, order):
        rows = mesh.shape["band"] * vectors.shape[2]
        square = (mesh.shape["band"], mesh.shape["vec"], vectors.shape[0], vectors.shape[2])
        if rows == band_cut.shape[0] and square == (GROUP,) * 4:
            return on_group(vectors, flow, band_cut, order)
        return on_device(vectors, flow, band_cut, order)

    return jax.shard_map(
        body, mesh=mesh, in_specs=in_specs, out_specs=out_specs, check_vma=False
    )
```
